32 devices in a mesh: clips: 2 (over y), tiles: 16 (over z, x, core).
Axes of the slice: x: 2, y: 2, z: 4, core: 2. Of those that a mesh axis runs over, the one named last changes fastest.
Arguments:
- frames: bfloat16 [4, 64, 256, 128], P(None, None, ('clips', 'tiles')), parts along dimension 2, may hold values from -6 to 6
- motion_forward: int32 [3, 512], P(None, ('clips', 'tiles')), parts along dimension 1, may hold values from 0 to 255, as said below
- motion_backward: int32 [3, 512], P(None, ('clips', 'tiles')), parts along dimension 1, may hold values from 0 to 255, as said below
- join_weight: bfloat16 [2, 64, 128], replicated, may hold values from -0.5 to 0.5
- conv_weight: bfloat16 [2, 4, 9, 64, 64], replicated, may hold values from -0.125 to 0.125
Outputs:
- forward_features: bfloat16 [4, 64, 256, 128], P(None, None, ('clips', 'tiles')), parts along dimension 2
- backward_features: bfloat16 [4, 64, 256, 128], P(None, None, ('clips', 'tiles')), parts along dimension 2
The draws below stay inside these ranges and needn't reach their ends.
There are 2 independent parts, one for each index of `clips`. The reference program is written for one: setup_inputs(seed, part) draws one part's arguments, and reference() takes and returns one part's arrays. A program takes and returns all parts, laid end to end along the dimension named above; an argument that names none is the same for every part. Nothing has to cross between parts.
Inputs may be any that keep to these rules, and one draw needn't show every extreme that they name: `motion_forward`: entries are block numbers of the frame; block number k lies in rows held by device k // 16. A block of device d takes a block of a device at most 2 away from d, at most two block columns to either side of its own column. Of the 16 blocks of one device, either none or exactly 4 take blocks of any one other device; in every frame some device takes 4 blocks from each device up to 2 away on both sides. `motion_backward`: entries are block numbers of the frame; block number k lies in rows held by device k // 16. A block of device d takes a block of a device at most 2 away from d, at most two block columns to either side of its own column. Of the 16 blocks of one device, either none or exactly 4 take blocks of any one other device; in every frame some device takes 4 blocks from each device up to 2 away on both sides.
All inputs are finite; a program needn't handle non-finite values.
Results may differ from the reference program's by a relative error of at most 0.018.
Values may be sent and summed in bfloat16 or wider, within the bound.
A program may use at most 64 MiB of HBM per device.

```python
import jax
import jax.numpy as jnp
from jax import lax

C = 64
ROWS_DEV = 8
COLS = 128
FRAMES = 4
CONVS = 4
BS = 8
REACH = 2
HEIGHT = 128
N_TILES = 16


def motion_lists(key, salt):
    block_count = ROWS_DEV // BS * (COLS // BS)
    capacity = block_count // (2 * REACH)
    block_rows = ROWS_DEV // BS
    block_cols = COLS // BS
    band_width = N_TILES // 8
    offset_table = jnp.array([offset for offset in range(-REACH, REACH + 1) if offset != 0], jnp.int32)
    frame_keys = jax.random.split(jax.random.fold_in(key, salt), FRAMES - 1)

    def one_frame(frame_key):
        center = jax.random.randint(jax.random.fold_in(frame_key, 1), (), 0, N_TILES)

        def one_device(device):
            device_key = jax.random.fold_in(frame_key, device + 7)
            fast_strip = jnp.abs(device - center) <= band_width
            slot_offset = jnp.repeat(offset_table, capacity)
            allowed = fast_strip | (jnp.abs(slot_offset) == 1)
            source_strip = device + slot_offset
            usable = allowed & (source_strip >= 0) & (source_strip < N_TILES)
            slot_offset = jnp.where(usable, slot_offset, 0)
            mixing = jax.random.permutation(jax.random.fold_in(device_key, 2), block_count)
            dest_offset = slot_offset[mixing]
            positions = jnp.arange(block_count).astype(jnp.int32)
            dest_col = positions % block_cols
            source_row = jax.random.randint(jax.random.fold_in(device_key, 3), (block_count,), 0, block_rows)
            drift = jax.random.randint(jax.random.fold_in(device_key, 4), (block_count,), -2, 3)
            source_col = jnp.clip(dest_col + drift, 0, block_cols - 1)
            return ((device + dest_offset) * block_count + source_row * block_cols + source_col).astype(jnp.int32)
        return jax.vmap(one_device)(jnp.arange(N_TILES).astype(jnp.int32)).reshape(-1)
    return jax.vmap(one_frame)(frame_keys)


def draw_motion_forward(key, part):
    return motion_lists(key, 11)


def draw_motion_backward(key, part):
    return motion_lists(key, 23)


def levels(rng, extent, cuts, smallest, high):
    def one(dim, shards_of):
        draws = jax.random.uniform(jax.random.fold_in(jax.random.fold_in(rng, 6), dim), (shards_of,), jnp.float32, smallest / len(cuts), high / len(cuts))
        return jnp.repeat(jnp.exp(draws), extent[dim] // shards_of).reshape((-1,) + (1,) * (len(extent) - dim - 1))

    factor_of = one(*cuts[0])
    for cut in cuts[1:]:
        factor_of = factor_of * one(*cut)
    return factor_of


def normal_values(stream_key, extent, width, limit, pieces=(), dtype=jnp.bfloat16):
    drawn = jax.random.normal(stream_key, extent, jnp.float32) * width
    if len(pieces) > 0:
        drawn = levels(stream_key, extent, pieces, -0.22, 0.18) * drawn
    return jnp.clip(drawn, min=-limit, max=limit).astype(dtype)


def setup_inputs(seed: int = 0, part: int = 0) -> dict:
    key_list = jax.random.split(jax.random.key(seed), 6)
    part_splits = jax.random.split(jax.random.fold_in(key_list[5], part), 6)
    frames = normal_values(part_splits[0], (FRAMES, C, HEIGHT, COLS), 1.0, 6.0, ((2, 16),))
    motion_forward = draw_motion_forward(jax.random.fold_in(jax.random.fold_in(key_list[5], part), 71), part)
    motion_backward = draw_motion_backward(jax.random.fold_in(jax.random.fold_in(key_list[5], part), 71), part)
    join_weight = normal_values(key_list[3], (2, C, 2 * C), (2 * C) ** -0.5, 0.5)
    conv_weight = normal_values(key_list[4], (2, CONVS, 9, C, C), (36 * C) ** -0.5, 0.125)
    return {"frames": frames, "motion_forward": motion_forward, "motion_backward": motion_backward, "join_weight": join_weight, "conv_weight": conv_weight}


def frame_blocks(field):
    channels, height, breadth = field.shape
    block_grid = field.reshape(channels, height // BS, BS, breadth // BS, BS)
    return block_grid.transpose(1, 3, 0, 2, 4).reshape(-1, channels * BS * BS)


def blocks_frame(blocks, channels, height, breadth):
    block_grid = blocks.reshape(height // BS, breadth // BS, channels, BS, BS)
    return block_grid.transpose(2, 0, 3, 1, 4).reshape(channels, height, breadth)


def refine(aligned, inputs, join_matrix, conv_layers):
    channels, height, breadth = inputs.shape
    mixed = jnp.einsum("oc,chw->ohw", join_matrix[:, :channels].astype(jnp.float32), aligned.astype(jnp.float32))
    mixed = mixed + jnp.einsum("oc,chw->ohw", join_matrix[:, channels:].astype(jnp.float32), inputs.astype(jnp.float32))
    carried = lax.optimization_barrier(mixed.astype(jnp.bfloat16))
    for layer_index in range(conv_layers.shape[0]):
        widened = carried.astype(jnp.float32)
        active = jnp.where(widened >= 0, widened, 0.1 * widened).astype(jnp.bfloat16)
        active = lax.optimization_barrier(active)
        padded = jnp.pad(active, ((0, 0), (1, 1), (1, 1))).astype(jnp.float32)
        summed = jnp.zeros(widened.shape, jnp.float32)
        for tap_index in range(9):
            row_shift = tap_index // 3
            column_shift = tap_index % 3
            window = padded[:, row_shift:row_shift + height, column_shift:column_shift + breadth]
            kernel = conv_layers[layer_index, tap_index].astype(jnp.float32)
            summed = summed + jnp.einsum("oi,ihw->ohw", kernel, window)
        carried = lax.optimization_barrier((widened + summed).astype(jnp.bfloat16))
    return carried


def reference(frames, motion_forward, motion_backward, join_weight, conv_weight):
    frame_total, channels, height, breadth = frames.shape
    forward = []
    carried = None
    for frame_time in range(frame_total):
        if frame_time == 0:
            aligned = jnp.zeros(frames.shape[1:], jnp.bfloat16)
        else:
            moved = jnp.take(frame_blocks(carried), motion_forward[frame_time - 1].astype(jnp.int32), axis=0)
            aligned = blocks_frame(moved, channels, height, breadth)
        carried = refine(aligned, frames[frame_time], join_weight[0], conv_weight[0])
        forward.append(carried)
    backward = []
    carried = None
    for frame_time in range(frame_total - 1, -1, -1):
        if frame_time == frame_total - 1:
            aligned = jnp.zeros(frames.shape[1:], jnp.bfloat16)
        else:
            moved = jnp.take(frame_blocks(carried), motion_backward[frame_time].astype(jnp.int32), axis=0)
            aligned = blocks_frame(moved, channels, height, breadth)
        carried = refine(aligned, frames[frame_time], join_weight[1], conv_weight[1])
        backward.append(carried)
    return jnp.stack(forward), jnp.stack(backward[::-1])
```

```python
import functools

import jax
import jax.numpy as jnp
from jax import lax
from jax.experimental import pallas as pl
from jax.experimental.pallas import tpu as pltpu
from jax.sharding import PartitionSpec as P

BS = 8
REACH = 2
OFFSETS = tuple(o for o in range(-REACH, REACH + 1) if o != 0)


def leaky(value):
    return jnp.maximum(value, 0.1 * value)


def blockdiag(tile):
    blank = jnp.zeros(tile.shape, tile.dtype)
    return jnp.concatenate(
        [jnp.concatenate([tile, blank], axis=1), jnp.concatenate([blank, tile], axis=1)], axis=0
    )


def matmul_t(left, right):
    return lax.dot_general(
        left, right, (((1,), (1,)), ((), ())), preferred_element_type=jnp.float32
    )


def sweep_kernel(
    dims,
    frames_hbm,
    mf_hbm,
    mb_hbm,
    join_hbm,
    conv_ref,
    ahead_ref,
    behind_ref,
    frames_ref,
    mf_ref,
    mb_ref,
    join_ref,
    conv_v,
    x_ref,
    flip,
    nat,
    wj_ref,
    wc_ref,
    mine,
    theirs,
    table_v,
    table_s,
    cand,
    packed,
    landed,
    h_ref,
    z_ref,
    edge_out,
    edge_in,
    m_send,
    m_recv,
    f_send,
    f_recv,
    e_send,
    e_recv,
    t_sem,
    w_sem,
    x_sem,
    i_sem,
):
    frame_count, rows, cols, channels, layers, devices = dims
    outs = (ahead_ref, behind_ref)
    lanes = 2 * channels
    half = cols // 2
    bc = cols // BS
    quad = BS // 2
    own_pairs = rows // 2
    margin = layers // 2
    all_pairs = own_pairs + 2 * margin
    cap = bc // (2 * REACH)
    sides = len(OFFSETS)
    lead = BS
    me = lax.axis_index("tiles")

    def present(offset):
        return (me + offset >= 0) & (me + offset < devices)

    def remote(source, target, send, receive, offset):
        return pltpu.make_async_remote_copy(
            src_ref=source,
            dst_ref=target,
            send_sem=send,
            recv_sem=receive,
            device_id={"tiles": me + offset},
            device_id_type=pl.DeviceIdType.MESH,
        )

    def motion_copy(oi, slot):
        return remote(mine, theirs.at[slot], m_send.at[oi], m_recv.at[slot], OFFSETS[oi])

    def feature_copy(d, step, oi, slot, offset):
        return remote(
            packed.at[d, step, oi], landed.at[d, step, slot],
            f_send.at[d, step, oi], f_recv.at[d, step, slot], offset,
        )

    def edge_copy(d, step, side, slot):
        return remote(
            edge_out.at[d, step, side], edge_in.at[d, step, slot],
            e_send.at[d, step, side], e_recv.at[d, step, slot], 1 if side else -1,
        )

    barrier = pltpu.get_barrier_semaphore()
    for offset in OFFSETS:
        @pl.when(present(offset))
        def _():
            pl.semaphore_signal(
                barrier, inc=1, device_id={"tiles": me + offset},
                device_id_type=pl.DeviceIdType.MESH,
            )

    first_frames = sorted({0, frame_count - 1})

    def frame_load(f):
        return pltpu.make_async_copy(frames_hbm.at[f], frames_ref.at[f], x_sem.at[f])

    small_loads = [
        pltpu.make_async_copy(source, target, i_sem.at[k])
        for k, (source, target) in enumerate(
            [(join_hbm, join_ref), (mf_hbm, mf_ref), (mb_hbm, mb_ref)]
        )
    ]
    weight_load = pltpu.make_async_copy(conv_ref, conv_v, w_sem)
    for f in first_frames:
        frame_load(f).start()
    for load in small_loads:
        load.start()
    weight_load.start()
    for f in range(1, frame_count - 1):
        frame_load(f).start()
    for oi, offset in enumerate(OFFSETS):
        @pl.when(jnp.logical_not(present(offset)))
        def _():
            theirs[oi] = jnp.full(mine.shape, -1, jnp.int32)

    for load in small_loads:
        load.wait()
    mine[...] = jnp.zeros(mine.shape, jnp.int32)
    for step in range(frame_count - 1):
        mine[step:step + 1, 0:bc] = mf_ref[step:step + 1, :]
        back = frame_count - 2 - step
        mine[frame_count - 1 + step:frame_count + step, 0:bc] = mb_ref[back:back + 1, :]

    for d in range(2):
        joined = join_ref[d]
        wj_ref[d, :, :lanes] = blockdiag(joined[:, :channels])
        wj_ref[d, :, lanes:] = blockdiag(joined[:, channels:])

    def load_frame(f):
        frame_load(f).wait()
        flip[0] = frames_ref[f].astype(jnp.float32).reshape(channels * rows, cols)
        parts = jnp.concatenate(
            [flip[0, pl.ds(r, channels, stride=rows), :] for r in range(rows)], axis=0
        ).astype(jnp.bfloat16)
        place = lax.broadcasted_iota(jnp.int32, (cols, cols), 0)
        column = lax.broadcasted_iota(jnp.int32, (cols, cols), 1)
        wanted = jnp.where(place < half, 2 * place, 2 * (place - half) + 1)
        moved = matmul_t((column == wanted).astype(jnp.bfloat16), parts).astype(jnp.bfloat16)
        for parity in range(2):
            for pair in range(own_pairs):
                x_ref[f, parity, pair * half:(pair + 1) * half, :] = moved[
                    parity * half:(parity + 1) * half, pair * lanes:(pair + 1) * lanes
                ]

    def build_weights(d):
        identity = (
            lax.broadcasted_iota(jnp.int32, (channels, channels), 0)
            == lax.broadcasted_iota(jnp.int32, (channels, channels), 1)
        ).astype(jnp.bfloat16)

        def build_layer(layer, carry):
            blank = jnp.zeros((channels, channels), jnp.bfloat16)
            for across in range(3):
                taps = [conv_v[d, layer, 3 * down + across] for down in range(3)]
                wide = jnp.concatenate(
                    [taps[0], blank, taps[1], taps[0], taps[2], taps[1], blank, taps[2]], axis=0
                )
                turned = matmul_t(identity, wide).astype(jnp.bfloat16)
                for k in range(4):
                    wc_ref[d, layer, across, k * channels:(k + 1) * channels, :] = turned[
                        :, k * lanes:(k + 1) * lanes
                    ]
            return carry

        lax.fori_loop(0, layers, build_layer, 0)

    def emit(t):
        identity = (
            lax.broadcasted_iota(jnp.int32, (lanes, lanes), 0)
            == lax.broadcasted_iota(jnp.int32, (lanes, lanes), 1)
        ).astype(jnp.bfloat16)
        for d in range(2):
            for pair in range(own_pairs):
                for parity in range(2):
                    nat[d, pl.ds(pair * cols + parity, half, stride=2), :] = cand[
                        d, 2 * pair + parity, lead:lead + half, :
                    ]
        moved = [matmul_t(identity, nat[d].astype(jnp.bfloat16)) for d in range(2)]
        for d in range(2):
            for pair in range(own_pairs):
                for low in range(2):
                    flip[d, pl.ds(2 * pair + low, channels, stride=rows), :] = moved[d][
                        low * channels:(low + 1) * channels, pair * cols:(pair + 1) * cols
                    ]
        for d in range(2):
            now = t if d == 0 else frame_count - 1 - t
            outs[d][now] = flip[d].reshape(channels, rows, cols).astype(jnp.bfloat16)

    def build_tables():
        for oi, offset in enumerate(OFFSETS):
            @pl.when(present(offset))
            def _():
                motion_copy(oi, oi).wait_send()
                motion_copy(oi, oi).wait_recv()

        depth = mine.shape[0]
        motion = mine[...]
        local = jnp.concatenate(
            [motion - (me + offset) * bc for offset in OFFSETS]
            + [theirs[oi] - me * bc for oi in range(sides)],
            axis=0,
        )
        lane = lax.broadcasted_iota(jnp.int32, local.shape, 1)
        match = (local >= 0) & (local < bc) & (lane < bc)
        flags = match.astype(jnp.int32)
        total = flags
        shift = 1
        while shift < bc:
            total = total + jnp.where(lane >= shift, pltpu.roll(total, shift, axis=1), 0)
            shift *= 2
        rank = total - flags

        mid = sides * depth
        own = motion - me * bc
        picks = jnp.where((own >= 0) & (own < bc), own, 0)
        for oi in range(sides):
            rows_of = slice(oi * depth, (oi + 1) * depth)
            code = bc + oi * cap + jnp.minimum(rank[rows_of], cap - 1)
            picks = picks + jnp.where(match[rows_of], code, 0)
        table_v[sides] = picks * quad

        wanted, order, chosen = local[mid:], rank[mid:], match[mid:]
        values = jnp.concatenate(
            [jnp.where(chosen & (order == slot), wanted, 0) for slot in range(cap)], axis=0
        )
        shift = 1
        while shift < bc + cap:
            values = values + pltpu.roll(values, shift, axis=1)
            shift *= 2
        place = lax.broadcasted_iota(jnp.int32, (mid, mine.shape[1]), 1)
        gathered = jnp.zeros(place.shape, jnp.int32)
        for slot in range(cap):
            gathered = jnp.where(place == bc + slot, values[slot * mid:(slot + 1) * mid], gathered)
        gathered = gathered * quad
        for oi in range(sides):
            table_v[oi] = gathered[oi * depth:(oi + 1) * depth]
        load = pltpu.make_async_copy(table_v, table_s, t_sem)
        load.start()
        load.wait()

    upper = lax.broadcasted_iota(jnp.int32, (BS, lanes), 0) < quad

    def two_blocks(d, k, first, second):
        return jnp.where(
            upper,
            cand[d, k, pl.ds(first + lead, BS), :],
            cand[d, k, pl.ds(second + lead - quad, BS), :],
        )

    def activate(d, slot, start, count, even, odd):
        first = start * half
        size = count * half
        z_ref[d, slot, 1, first:first + size, :] = even.astype(jnp.bfloat16)
        z_ref[d, slot, 2, first:first + size, :] = odd.astype(jnp.bfloat16)
        place = lax.broadcasted_iota(jnp.int32, (count, BS, lanes), 1)
        before = pltpu.roll(odd.reshape(count, half, lanes), 1, axis=1)
        before = jnp.concatenate(
            [jnp.where(place == 0, 0.0, before[:, :BS]), before[:, BS:]], axis=1
        )
        z_ref[d, slot, 0, first:first + size, :] = before.reshape(size, lanes).astype(jnp.bfloat16)
        after = pltpu.roll(even.reshape(count, half, lanes), half - 1, axis=1)
        after = jnp.concatenate(
            [after[:, :half - BS], jnp.where(place == BS - 1, 0.0, after[:, half - BS:])], axis=1
        )
        z_ref[d, slot, 3, first:first + size, :] = after.reshape(size, lanes).astype(jnp.bfloat16)

    def send_edges(d, t, first):
        size = own_pairs * half
        edge = margin * half
        for parity in range(2):
            base = parity * size
            edge_out[d, t, 0, parity] = first[base:base + edge]
            edge_out[d, t, 1, parity] = first[base + size - edge:base + size]
        for side in range(2):
            @pl.when(present(1 if side else -1))
            def _():
                edge_copy(d, t, side, 1 - side).start()
        wide = first.astype(jnp.float32)
        h_ref[d, 0, 0, edge:edge + size, :] = wide[:size]
        h_ref[d, 0, 1, edge:edge + size, :] = wide[size:]
        wide = leaky(wide)
        activate(d, 0, margin, own_pairs, wide[:size], wide[size:])

    def begin_first(d):
        now = 0 if d == 0 else frame_count - 1
        both = jnp.concatenate([x_ref[now, 0], x_ref[now, 1]], axis=0)
        send_edges(d, 0, matmul_t(both, wj_ref[d, :, lanes:]).astype(jnp.bfloat16))

    def begin(d, t):
        step = t - 1
        row = d * (frame_count - 1) + step
        for oi, offset in enumerate(OFFSETS):
            @pl.when(present(offset))
            def _():
                feature_copy(d, step, oi, oi, offset).wait_recv()
                at = lead + (bc + oi * cap) * quad
                for k in range(2 * own_pairs):
                    cand[d, k, at:at + cap * quad, :] = landed[d, step, oi, k].astype(jnp.float32)
        picks = [table_s[sides, row, j] for j in range(bc)]
        now = t if d == 0 else frame_count - 1 - t
        parts = []
        for parity in range(2):
            tiles = [
                two_blocks(d, 2 * pair + parity, picks[2 * j], picks[2 * j + 1])
                for pair in range(own_pairs)
                for j in range(bc // 2)
            ]
            taken = jnp.concatenate(tiles, axis=0).astype(jnp.bfloat16)
            parts.append(jnp.concatenate([taken, x_ref[now, parity]], axis=1))
        both = jnp.concatenate(parts, axis=0)
        send_edges(d, t, matmul_t(both, wj_ref[d]).astype(jnp.bfloat16))

    top_inside = (me > 0).astype(jnp.float32)
    bottom_inside = (me < devices - 1).astype(jnp.float32)

    low_lanes = lax.broadcasted_iota(jnp.int32, (1, lanes), 1) < channels
    top_mixed = jnp.where(low_lanes, top_inside, 1.0)
    bottom_mixed = jnp.where(low_lanes, 1.0, bottom_inside)

    def inside(value, layer, begin_pair):
        count = value.shape[0] // half
        pieces = []
        for q in range(count):
            start = 2 * (q + begin_pair) + layer + 1 - layers
            piece = value[q * half:(q + 1) * half]
            if start + 1 < 0:
                piece = piece * top_inside
            elif start < 0:
                piece = piece * top_mixed
            elif start >= rows:
                piece = piece * bottom_inside
            elif start + 1 >= rows:
                piece = piece * bottom_mixed
            pieces.append(piece)
        return jnp.concatenate(pieces, axis=0)

    def multiply(d, layer, first, last):
        now = layer % 2
        base = first * half
        size = (last - first) * half
        left = jnp.concatenate(
            [
                z_ref[d, now, k, base + low * half:base + low * half + size, :]
                for k in range(4)
                for low in range(2)
            ],
            axis=1,
        )
        taps = [wc_ref[d, layer, across] for across in range(3)]
        blank = jnp.zeros(taps[0].shape, jnp.bfloat16)
        right = jnp.concatenate(
            [
                jnp.concatenate([taps[0], blank], axis=1),
                jnp.concatenate([taps[1], taps[0]], axis=1),
                jnp.concatenate([taps[2], taps[1]], axis=1),
                jnp.concatenate([blank, taps[2]], axis=1),
            ],
            axis=0,
        )
        return jnp.dot(left, right, preferred_element_type=jnp.float32)

    def settle(d, layer, first, last, summed):
        now, later = layer % 2, (layer + 1) % 2
        count = last - first
        base = first * half
        size = count * half
        first_half = lax.broadcasted_iota(jnp.int32, (size, lanes), 1) < channels
        fresh = []
        for parity in range(2):
            kept = jnp.where(
                first_half,
                h_ref[d, now, parity, base + half:base + half + size, :],
                h_ref[d, now, parity, base:base + size, :],
            )
            fresh.append(
                pltpu.roll(kept, channels, axis=1) + summed[:, parity * lanes:(parity + 1) * lanes]
            )
        if layer < layers - 1:
            for parity in range(2):
                h_ref[d, later, parity, base:base + size, :] = fresh[parity]
            activate(
                d, later, first, count,
                inside(leaky(fresh[0]), layer, first), inside(leaky(fresh[1]), layer, first),
            )
        else:
            for parity in range(2):
                rounded = fresh[parity].astype(jnp.bfloat16).astype(jnp.float32)
                for pair in range(first, last):
                    at = (pair - first) * half
                    cand[d, 2 * pair + parity, lead:lead + half, :] = rounded[at:at + half]

    def finish(d, t):
        edge = margin * half
        for side in range(2):
            pair = side * (margin + own_pairs)
            start = pair * half

            @pl.when(present(1 if side else -1))
            def _():
                edge_copy(d, t, side, side).wait_recv()
                even = edge_in[d, t, side, 0].astype(jnp.float32)
                odd = edge_in[d, t, side, 1].astype(jnp.float32)
                h_ref[d, 0, 0, start:start + edge, :] = even
                h_ref[d, 0, 1, start:start + edge, :] = odd
                activate(d, 0, pair, margin, leaky(even), leaky(odd))

            @pl.when(jnp.logical_not(present(1 if side else -1)))
            def _():
                for parity in range(2):
                    h_ref[d, 0, parity, start:start + edge, :] = jnp.zeros((edge, lanes), jnp.float32)
                for k in range(4):
                    z_ref[d, 0, k, start:start + edge, :] = jnp.zeros((edge, lanes), jnp.bfloat16)

        for layer in range(layers):
            settle(d, layer, 0, all_pairs - 1 - layer, multiply(d, layer, 0, all_pairs - 1 - layer))

        @pl.when(t < frame_count - 1)
        def _():
            row = d * (frame_count - 1) + t
            for oi, offset in enumerate(OFFSETS):
                picks = [table_s[oi, row, bc + slot] for slot in range(cap)]
                for k in range(2 * own_pairs):
                    packed[d, t, oi, k] = jnp.concatenate(
                        [
                            two_blocks(d, k, picks[slot], picks[slot + 1])
                            for slot in range(0, cap, 2)
                        ],
                        axis=0,
                    ).astype(jnp.bfloat16)
            flag = (me // 2) % 2
            for k in range(sides):
                oi = k + flag * (sides - 1 - 2 * k)
                offset = oi - REACH + (oi + REACH) // (2 * REACH)

                @pl.when(present(offset))
                def _():
                    feature_copy(d, t, oi, sides - 1 - oi, offset).start()

    for f in first_frames:
        load_frame(f)

    peers = jnp.minimum(me, REACH) + jnp.minimum(devices - 1 - me, REACH)
    pl.semaphore_wait(barrier, peers)

    for oi, offset in enumerate(OFFSETS):
        @pl.when(present(offset))
        def _():
            motion_copy(oi, sides - 1 - oi).start()
    for d in range(2):
        begin_first(d)

    def load_rest(f, carry):
        load_frame(f)
        return carry

    lax.fori_loop(1, frame_count - 1, load_rest, 0)
    weight_load.wait()
    for d in range(2):
        build_weights(d)
    build_tables()

    def frame_step(t, carry):
        finish(0, t)
        finish(1, t)
        emit(t)

        @pl.when(t < frame_count - 1)
        def _():
            begin(0, t + 1)
            begin(1, t + 1)

        return carry

    lax.fori_loop(0, frame_count, frame_step, 0)

    for d in range(2):
        for step in range(frame_count):
            for side in range(2):
                @pl.when(present(1 if side else -1))
                def _():
                    edge_copy(d, step, side, side).wait_send()
            if step < frame_count - 1:
                for oi, offset in enumerate(OFFSETS):
                    @pl.when(present(offset))
                    def _():
                        feature_copy(d, step, oi, oi, offset).wait_send()


def on_device(frames, motion_forward, motion_backward, join_weight, conv_weight):
    frame_count, channels, rows, cols = frames.shape
    layers = conv_weight.shape[1]
    devices = lax.axis_size("tiles")
    lanes = 2 * channels
    half = cols // 2
    bc = rows // BS * (cols // BS)
    cap = bc // (2 * REACH)
    sides = len(OFFSETS)
    steps = frame_count - 1
    own_pairs = rows // 2
    margin = layers // 2
    all_pairs = own_pairs + 2 * margin
    quad = BS // 2
    reach = 2 * BS + (bc + sides * cap) * quad

    dims = (frame_count, rows, cols, channels, layers, devices)
    vmem = pl.BlockSpec(memory_space=pltpu.VMEM)
    result = pltpu.VMEM(frames.shape, jnp.bfloat16)
    block = (2 * own_pairs, cap * quad, lanes)
    edge = (2, margin * half, lanes)
    return pl.pallas_call(
        functools.partial(sweep_kernel, dims),
        out_shape=(result, result),
        in_specs=[pl.BlockSpec(memory_space=pltpu.HBM)] * 5,
        out_specs=(vmem, vmem),
        scratch_shapes=[
            pltpu.VMEM(frames.shape, jnp.bfloat16),
            pltpu.VMEM(motion_forward.shape, jnp.int32),
            pltpu.VMEM(motion_backward.shape, jnp.int32),
            pltpu.VMEM(join_weight.shape, jnp.bfloat16),
            pltpu.VMEM(conv_weight.shape, jnp.bfloat16),
            pltpu.VMEM((frame_count, 2, own_pairs * half, lanes), jnp.bfloat16),
            pltpu.VMEM((2, channels * rows, cols), jnp.float32),
            pltpu.VMEM((2, own_pairs * cols, lanes), jnp.float32),
            pltpu.VMEM((2, lanes, 2 * lanes), jnp.bfloat16),
            pltpu.VMEM((2, layers, 3, 2 * lanes, lanes), jnp.bfloat16),
            pltpu.VMEM((8, 128), jnp.int32),
            pltpu.VMEM((sides, 8, 128), jnp.int32),
            pltpu.VMEM((sides + 1, 8, 128), jnp.int32),
            pltpu.SMEM((sides + 1, 8, 128), jnp.int32),
            pltpu.VMEM((2, 2 * own_pairs, reach, lanes), jnp.float32),
            pltpu.VMEM((2, steps, sides, *block), jnp.bfloat16),
            pltpu.VMEM((2, steps, sides, *block), jnp.bfloat16),
            pltpu.VMEM((2, 2, 2, all_pairs * half, lanes), jnp.float32),
            pltpu.VMEM((2, 2, 4, all_pairs * half, lanes), jnp.bfloat16),
            pltpu.VMEM((2, frame_count, 2, *edge), jnp.bfloat16),
            pltpu.VMEM((2, frame_count, 2, *edge), jnp.bfloat16),
            pltpu.SemaphoreType.DMA((sides,)),
            pltpu.SemaphoreType.DMA((sides,)),
            pltpu.SemaphoreType.DMA((2, steps, sides)),
            pltpu.SemaphoreType.DMA((2, steps, sides)),
            pltpu.SemaphoreType.DMA((2, frame_count, 2)),
            pltpu.SemaphoreType.DMA((2, frame_count, 2)),
            pltpu.SemaphoreType.DMA,
            pltpu.SemaphoreType.DMA,
            pltpu.SemaphoreType.DMA((frame_count,)),
            pltpu.SemaphoreType.DMA((3,)),
        ],
        compiler_params=pltpu.CompilerParams(
            collective_id=0, has_side_effects=True, vmem_limit_bytes=60 * 1024 * 1024
        ),
    )(frames, motion_forward, motion_backward, join_weight, conv_weight)


def solution(mesh):
    return jax.shard_map(
        on_device,
        mesh=mesh,
        in_specs=(
            P(None, None, ("clips", "tiles"), None),
            P(None, ("clips", "tiles")),
            P(None, ("clips", "tiles")),
            P(),
            P(),
        ),
        out_specs=(
            P(None, None, ("clips", "tiles"), None),
            P(None, None, ("clips", "tiles"), None),
        ),
        check_vma=False,
    )
```

```python
import functools

import jax
import jax.numpy as jnp
from jax import lax
from jax.experimental import pallas as pl
from jax.experimental.pallas import tpu as pltpu
from jax.sharding import PartitionSpec as P

BS = 8
REACH = 2
OFFSETS = tuple(o for o in range(-REACH, REACH + 1) if o != 0)


def leaky(value):
    return jnp.maximum(value, 0.1 * value)


def blockdiag(tile):
    blank = jnp.zeros(tile.shape, tile.dtype)
    return jnp.concatenate(
        [jnp.concatenate([tile, blank], axis=1), jnp.concatenate([blank, tile], axis=1)], axis=0
    )


def matmul_t(left, right):
    return lax.dot_general(
        left, right, (((1,), (1,)), ((), ())), preferred_element_type=jnp.float32
    )


def sweep_kernel(
    dims,
    frames_hbm,
    mf_hbm,
    mb_hbm,
    join_hbm,
    conv_ref,
    ahead_ref,
    behind_ref,
    frames_ref,
    mf_ref,
    mb_ref,
    join_ref,
    conv_v,
    x_ref,
    flip,
    nat,
    wj_ref,
    wc_ref,
    mine,
    theirs,
    table_v,
    table_s,
    cand,
    packed,
    landed,
    h_ref,
    z_ref,
    edge_out,
    edge_in,
    m_send,
    f_send,
    f_recv,
    e_send,
    e_recv,
    x_sem,
):
    frame_count, rows, cols, channels, layers, devices = dims
    outs = (ahead_ref, behind_ref)
    lanes = 2 * channels
    half = cols // 2
    bc = cols // BS
    quad = BS // 2
    own_pairs = rows // 2
    margin = layers // 2
    all_pairs = own_pairs + 2 * margin
    cap = bc // (2 * REACH)
    sides = len(OFFSETS)
    lead = BS
    me = lax.axis_index("tiles")

    def present(offset):
        return (me + offset >= 0) & (me + offset < devices)

    def remote(source, target, send, receive, offset):
        return pltpu.make_async_remote_copy(
            src_ref=source,
            dst_ref=target,
            send_sem=send,
            recv_sem=receive,
            device_id={"tiles": me + offset},
            device_id_type=pl.DeviceIdType.MESH,
        )

    def motion_copy(oi, slot):
        return remote(mine, theirs.at[slot], m_send.at[oi], f_recv.at[1, 1, slot], OFFSETS[oi])

    def feature_copy(d, step, oi, slot, offset):
        return remote(
            packed.at[d, step, oi], landed.at[d, step, slot],
            f_send.at[d, oi], f_recv.at[d, step % 2, slot], offset,
        )

    def edge_copy(d, step, side, slot):
        return remote(
            edge_out.at[d, step, side], edge_in.at[d, step, slot],
            e_send.at[d, side], e_recv.at[d, slot], 1 if side else -1,
        )

    barrier = pltpu.get_barrier_semaphore()
    for offset in OFFSETS:
        @pl.when(present(offset))
        def _():
            pl.semaphore_signal(
                barrier, inc=1, device_id={"tiles": me + offset},
                device_id_type=pl.DeviceIdType.MESH,
            )

    first_frames = sorted({0, frame_count - 1})

    def frame_load(f):
        return pltpu.make_async_copy(frames_hbm.at[f], frames_ref.at[f], x_sem.at[f])

    small_loads = [
        pltpu.make_async_copy(source, target, f_send.at[1, k])
        for k, (source, target) in enumerate(
            [(join_hbm, join_ref), (mf_hbm, mf_ref), (mb_hbm, mb_ref)]
        )
    ]
    weight_load = pltpu.make_async_copy(conv_ref, conv_v, f_send.at[0, 0])
    for f in first_frames:
        frame_load(f).start()
    for load in small_loads:
        load.start()
    weight_load.start()
    for f in range(1, frame_count - 1):
        frame_load(f).start()
    for oi, offset in enumerate(OFFSETS):
        @pl.when(jnp.logical_not(present(offset)))
        def _():
            theirs[oi] = jnp.full(mine.shape, -1, jnp.int32)

    for load in small_loads:
        load.wait()
    mine[...] = jnp.zeros(mine.shape, jnp.int32)
    for step in range(frame_count - 1):
        mine[step:step + 1, 0:bc] = mf_ref[step:step + 1, :]
        back = frame_count - 2 - step
        mine[frame_count - 1 + step:frame_count + step, 0:bc] = mb_ref[back:back + 1, :]

    for d in range(2):
        joined = join_ref[d]
        wj_ref[d, :, :lanes] = blockdiag(joined[:, :channels])
        wj_ref[d, :, lanes:] = blockdiag(joined[:, channels:])

    def load_frame(f):
        frame_load(f).wait()
        flip[0] = frames_ref[f].astype(jnp.float32).reshape(channels * rows, cols)
        parts = jnp.concatenate(
            [flip[0, pl.ds(r, channels, stride=rows), :] for r in range(rows)], axis=0
        ).astype(jnp.bfloat16)
        place = lax.broadcasted_iota(jnp.int32, (cols, cols), 0)
        column = lax.broadcasted_iota(jnp.int32, (cols, cols), 1)
        wanted = jnp.where(place < half, 2 * place, 2 * (place - half) + 1)
        moved = matmul_t((column == wanted).astype(jnp.bfloat16), parts).astype(jnp.bfloat16)
        for parity in range(2):
            for pair in range(own_pairs):
                x_ref[f, parity, pair * half:(pair + 1) * half, :] = moved[
                    parity * half:(parity + 1) * half, pair * lanes:(pair + 1) * lanes
                ]

    def build_weights(d):
        identity = (
            lax.broadcasted_iota(jnp.int32, (channels, channels), 0)
            == lax.broadcasted_iota(jnp.int32, (channels, channels), 1)
        ).astype(jnp.bfloat16)

        def build_layer(layer, carry):
            blank = jnp.zeros((channels, channels), jnp.bfloat16)
            for across in range(3):
                taps = [conv_v[d, layer, 3 * down + across] for down in range(3)]
                wide = jnp.concatenate(
                    [taps[0], blank, taps[1], taps[0], taps[2], taps[1], blank, taps[2]], axis=0
                )
                turned = matmul_t(identity, wide).astype(jnp.bfloat16)
                for k in range(4):
                    wc_ref[d, layer, across, k * channels:(k + 1) * channels, :] = turned[
                        :, k * lanes:(k + 1) * lanes
                    ]
            return carry

        lax.fori_loop(0, layers, build_layer, 0)

    def emit(t):
        identity = (
            lax.broadcasted_iota(jnp.int32, (lanes, lanes), 0)
            == lax.broadcasted_iota(jnp.int32, (lanes, lanes), 1)
        ).astype(jnp.bfloat16)
        for d in range(2):
            for pair in range(own_pairs):
                for parity in range(2):
                    nat[d, pl.ds(pair * cols + parity, half, stride=2), :] = cand[
                        d, 2 * pair + parity, lead:lead + half, :
                    ]
        moved = [matmul_t(identity, nat[d].astype(jnp.bfloat16)) for d in range(2)]
        for d in range(2):
            for pair in range(own_pairs):
                for low in range(2):
                    flip[d, pl.ds(2 * pair + low, channels, stride=rows), :] = moved[d][
                        low * channels:(low + 1) * channels, pair * cols:(pair + 1) * cols
                    ]
        for d in range(2):
            now = t if d == 0 else frame_count - 1 - t
            outs[d][now] = flip[d].reshape(channels, rows, cols).astype(jnp.bfloat16)

    def build_tables():
        for oi, offset in enumerate(OFFSETS):
            @pl.when(present(offset))
            def _():
                motion_copy(oi, oi).wait_send()
                motion_copy(oi, oi).wait_recv()

        depth = mine.shape[0]
        motion = mine[...]
        local = jnp.concatenate(
            [motion - (me + offset) * bc for offset in OFFSETS]
            + [theirs[oi] - me * bc for oi in range(sides)],
            axis=0,
        )
        lane = lax.broadcasted_iota(jnp.int32, local.shape, 1)
        match = (local >= 0) & (local < bc) & (lane < bc)
        flags = match.astype(jnp.int32)
        total = flags
        shift = 1
        while shift < bc:
            total = total + jnp.where(lane >= shift, pltpu.roll(total, shift, axis=1), 0)
            shift *= 2
        rank = total - flags

        mid = sides * depth
        own = motion - me * bc
        picks = jnp.where((own >= 0) & (own < bc), own, 0)
        for oi in range(sides):
            rows_of = slice(oi * depth, (oi + 1) * depth)
            code = bc + oi * cap + jnp.minimum(rank[rows_of], cap - 1)
            picks = picks + jnp.where(match[rows_of], code, 0)
        table_v[sides] = picks * quad

        wanted, order, chosen = local[mid:], rank[mid:], match[mid:]
        values = jnp.concatenate(
            [jnp.where(chosen & (order == slot), wanted, 0) for slot in range(cap)], axis=0
        )
        shift = 1
        while shift < bc + cap:
            values = values + pltpu.roll(values, shift, axis=1)
            shift *= 2
        place = lax.broadcasted_iota(jnp.int32, (mid, mine.shape[1]), 1)
        gathered = jnp.zeros(place.shape, jnp.int32)
        for slot in range(cap):
            gathered = jnp.where(place == bc + slot, values[slot * mid:(slot + 1) * mid], gathered)
        gathered = gathered * quad
        for oi in range(sides):
            table_v[oi] = gathered[oi * depth:(oi + 1) * depth]
        load = pltpu.make_async_copy(table_v, table_s, f_send.at[0, 1])
        load.start()
        load.wait()

    upper = lax.broadcasted_iota(jnp.int32, (BS, lanes), 0) < quad

    def two_blocks(d, k, first, second):
        return jnp.where(
            upper,
            cand[d, k, pl.ds(first + lead, BS), :],
            cand[d, k, pl.ds(second + lead - quad, BS), :],
        )

    def activate(d, slot, start, count, even, odd):
        first = start * half
        size = count * half
        z_ref[d, slot, 1, first:first + size, :] = even.astype(jnp.bfloat16)
        z_ref[d, slot, 2, first:first + size, :] = odd.astype(jnp.bfloat16)
        place = lax.broadcasted_iota(jnp.int32, (count, BS, lanes), 1)
        before = pltpu.roll(odd.reshape(count, half, lanes), 1, axis=1)
        before = jnp.concatenate(
            [jnp.where(place == 0, 0.0, before[:, :BS]), before[:, BS:]], axis=1
        )
        z_ref[d, slot, 0, first:first + size, :] = before.reshape(size, lanes).astype(jnp.bfloat16)
        after = pltpu.roll(even.reshape(count, half, lanes), half - 1, axis=1)
        after = jnp.concatenate(
            [after[:, :half - BS], jnp.where(place == BS - 1, 0.0, after[:, half - BS:])], axis=1
        )
        z_ref[d, slot, 3, first:first + size, :] = after.reshape(size, lanes).astype(jnp.bfloat16)

    def send_edges(d, t, first):
        size = own_pairs * half
        edge = margin * half
        for parity in range(2):
            base = parity * size
            edge_out[d, t, 0, parity] = first[base:base + edge]
            edge_out[d, t, 1, parity] = first[base + size - edge:base + size]
        for side in range(2):
            @pl.when(present(1 if side else -1))
            def _():
                edge_copy(d, t, side, 1 - side).start()
        wide = first.astype(jnp.float32)
        h_ref[d, 0, 0, edge:edge + size, :] = wide[:size]
        h_ref[d, 0, 1, edge:edge + size, :] = wide[size:]
        wide = leaky(wide)
        activate(d, 0, margin, own_pairs, wide[:size], wide[size:])

    def begin_first(d):
        now = 0 if d == 0 else frame_count - 1
        both = jnp.concatenate([x_ref[now, 0], x_ref[now, 1]], axis=0)
        send_edges(d, 0, matmul_t(both, wj_ref[d, :, lanes:]).astype(jnp.bfloat16))

    def begin(d, t):
        step = t - 1
        row = d * (frame_count - 1) + step
        for oi, offset in enumerate(OFFSETS):
            @pl.when(present(offset))
            def _():
                feature_copy(d, step, oi, oi, offset).wait_recv()
                at = lead + (bc + oi * cap) * quad
                for k in range(2 * own_pairs):
                    cand[d, k, at:at + cap * quad, :] = landed[d, step, oi, k].astype(jnp.float32)
        picks = [table_s[sides, row, j] for j in range(bc)]
        now = t if d == 0 else frame_count - 1 - t
        parts = []
        for parity in range(2):
            tiles = [
                two_blocks(d, 2 * pair + parity, picks[2 * j], picks[2 * j + 1])
                for pair in range(own_pairs)
                for j in range(bc // 2)
            ]
            taken = jnp.concatenate(tiles, axis=0).astype(jnp.bfloat16)
            parts.append(jnp.concatenate([taken, x_ref[now, parity]], axis=1))
        both = jnp.concatenate(parts, axis=0)
        send_edges(d, t, matmul_t(both, wj_ref[d]).astype(jnp.bfloat16))
        for oi, offset in enumerate(OFFSETS):
            @pl.when(present(offset))
            def _():
                feature_copy(d, step, oi, oi, offset).wait_send()

    top_inside = (me > 0).astype(jnp.float32)
    bottom_inside = (me < devices - 1).astype(jnp.float32)

    low_lanes = lax.broadcasted_iota(jnp.int32, (1, lanes), 1) < channels
    top_mixed = jnp.where(low_lanes, top_inside, 1.0)
    bottom_mixed = jnp.where(low_lanes, 1.0, bottom_inside)

    def inside(value, layer, begin_pair):
        count = value.shape[0] // half
        pieces = []
        for q in range(count):
            start = 2 * (q + begin_pair) + layer + 1 - layers
            piece = value[q * half:(q + 1) * half]
            if start + 1 < 0:
                piece = piece * top_inside
            elif start < 0:
                piece = piece * top_mixed
            elif start >= rows:
                piece = piece * bottom_inside
            elif start + 1 >= rows:
                piece = piece * bottom_mixed
            pieces.append(piece)
        return jnp.concatenate(pieces, axis=0)

    def multiply(d, layer, first, last):
        now = layer % 2
        base = first * half
        size = (last - first) * half
        left = jnp.concatenate(
            [
                z_ref[d, now, k, base + low * half:base + low * half + size, :]
                for k in range(4)
                for low in range(2)
            ],
            axis=1,
        )
        taps = [wc_ref[d, layer, across] for across in range(3)]
        blank = jnp.zeros(taps[0].shape, jnp.bfloat16)
        right = jnp.concatenate(
            [
                jnp.concatenate([taps[0], blank], axis=1),
                jnp.concatenate([taps[1], taps[0]], axis=1),
                jnp.concatenate([taps[2], taps[1]], axis=1),
                jnp.concatenate([blank, taps[2]], axis=1),
            ],
            axis=0,
        )
        return jnp.dot(left, right, preferred_element_type=jnp.float32)

    def settle(d, layer, first, last, summed):
        now, later = layer % 2, (layer + 1) % 2
        count = last - first
        base = first * half
        size = count * half
        first_half = lax.broadcasted_iota(jnp.int32, (size, lanes), 1) < channels
        fresh = []
        for parity in range(2):
            kept = jnp.where(
                first_half,
                h_ref[d, now, parity, base + half:base + half + size, :],
                h_ref[d, now, parity, base:base + size, :],
            )
            fresh.append(
                pltpu.roll(kept, channels, axis=1) + summed[:, parity * lanes:(parity + 1) * lanes]
            )
        if layer < layers - 1:
            for parity in range(2):
                h_ref[d, later, parity, base:base + size, :] = fresh[parity]
            activate(
                d, later, first, count,
                inside(leaky(fresh[0]), layer, first), inside(leaky(fresh[1]), layer, first),
            )
        else:
            for parity in range(2):
                rounded = fresh[parity].astype(jnp.bfloat16).astype(jnp.float32)
                for pair in range(first, last):
                    at = (pair - first) * half
                    cand[d, 2 * pair + parity, lead:lead + half, :] = rounded[at:at + half]

    def finish(d, t):
        edge = margin * half
        for side in range(2):
            pair = side * (margin + own_pairs)
            start = pair * half

            @pl.when(present(1 if side else -1))
            def _():
                edge_copy(d, t, side, side).wait_recv()
                even = edge_in[d, t, side, 0].astype(jnp.float32)
                odd = edge_in[d, t, side, 1].astype(jnp.float32)
                h_ref[d, 0, 0, start:start + edge, :] = even
                h_ref[d, 0, 1, start:start + edge, :] = odd
                activate(d, 0, pair, margin, leaky(even), leaky(odd))

            @pl.when(jnp.logical_not(present(1 if side else -1)))
            def _():
                for parity in range(2):
                    h_ref[d, 0, parity, start:start + edge, :] = jnp.zeros((edge, lanes), jnp.float32)
                for k in range(4):
                    z_ref[d, 0, k, start:start + edge, :] = jnp.zeros((edge, lanes), jnp.bfloat16)

        spans = []
        for layer in range(layers):
            split = layers - layer
            spans += [(layer, 0, split), (layer, split, all_pairs - 1 - layer)]
        pending = [multiply(d, *spans[0])]
        for k, span in enumerate(spans):
            if k + 1 < len(spans):
                pending.append(multiply(d, *spans[k + 1]))
            settle(d, *span, pending[k])

        @pl.when(t < frame_count - 1)
        def _():
            row = d * (frame_count - 1) + t
            for oi, offset in enumerate(OFFSETS):
                picks = [table_s[oi, row, bc + slot] for slot in range(cap)]
                for k in range(2 * own_pairs):
                    packed[d, t, oi, k] = jnp.concatenate(
                        [
                            two_blocks(d, k, picks[slot], picks[slot + 1])
                            for slot in range(0, cap, 2)
                        ],
                        axis=0,
                    ).astype(jnp.bfloat16)
            flag = (me // 2) % 2
            for k in range(sides):
                oi = k + flag * (sides - 1 - 2 * k)
                offset = oi - REACH + (oi + REACH) // (2 * REACH)

                @pl.when(present(offset))
                def _():
                    feature_copy(d, t, oi, sides - 1 - oi, offset).start()

        for side in range(2):
            @pl.when(present(1 if side else -1))
            def _():
                edge_copy(d, t, side, side).wait_send()

    for f in first_frames:
        load_frame(f)

    peers = jnp.minimum(me, REACH) + jnp.minimum(devices - 1 - me, REACH)
    pl.semaphore_wait(barrier, peers)

    for oi, offset in enumerate(OFFSETS):
        @pl.when(present(offset))
        def _():
            motion_copy(oi, sides - 1 - oi).start()
    for d in range(2):
        begin_first(d)

    def load_rest(f, carry):
        load_frame(f)
        return carry

    lax.fori_loop(1, frame_count - 1, load_rest, 0)
    weight_load.wait()
    for d in range(2):
        build_weights(d)
    build_tables()

    def frame_step(t, carry):
        finish(0, t)
        finish(1, t)
        emit(t)

        @pl.when(t < frame_count - 1)
        def _():
            begin(0, t + 1)
            begin(1, t + 1)

        return carry

    lax.fori_loop(0, frame_count, frame_step, 0)


def store_kernel(ahead_ref, behind_ref, ahead_out, behind_out, sems):
    copies = [
        pltpu.make_async_copy(source.at[f], target.at[f], sems.at[k, f])
        for k, (source, target) in enumerate([(ahead_ref, ahead_out), (behind_ref, behind_out)])
        for f in range(source.shape[0])
    ]
    for copy in copies:
        copy.start()
    for copy in copies:
        copy.wait()


def on_device(frames, motion_forward, motion_backward, join_weight, conv_weight):
    frame_count, channels, rows, cols = frames.shape
    layers = conv_weight.shape[1]
    devices = lax.axis_size("tiles")
    lanes = 2 * channels
    half = cols // 2
    bc = rows // BS * (cols // BS)
    cap = bc // (2 * REACH)
    sides = len(OFFSETS)
    steps = frame_count - 1
    own_pairs = rows // 2
    margin = layers // 2
    all_pairs = own_pairs + 2 * margin
    quad = BS // 2
    reach = 2 * BS + (bc + sides * cap) * quad

    dims = (frame_count, rows, cols, channels, layers, devices)
    vmem = pl.BlockSpec(memory_space=pltpu.VMEM)
    result = pltpu.VMEM(frames.shape, jnp.bfloat16)
    block = (2 * own_pairs, cap * quad, lanes)
    edge = (2, margin * half, lanes)
    swept = pl.pallas_call(
        functools.partial(sweep_kernel, dims),
        out_shape=(result, result),
        in_specs=[pl.BlockSpec(memory_space=pltpu.HBM)] * 5,
        out_specs=(vmem, vmem),
        scratch_shapes=[
            pltpu.VMEM(frames.shape, jnp.bfloat16),
            pltpu.VMEM(motion_forward.shape, jnp.int32),
            pltpu.VMEM(motion_backward.shape, jnp.int32),
            pltpu.VMEM(join_weight.shape, jnp.bfloat16),
            pltpu.VMEM(conv_weight.shape, jnp.bfloat16),
            pltpu.VMEM((frame_count, 2, own_pairs * half, lanes), jnp.bfloat16),
            pltpu.VMEM((2, channels * rows, cols), jnp.float32),
            pltpu.VMEM((2, own_pairs * cols, lanes), jnp.float32),
            pltpu.VMEM((2, lanes, 2 * lanes), jnp.bfloat16),
            pltpu.VMEM((2, layers, 3, 2 * lanes, lanes), jnp.bfloat16),
            pltpu.VMEM((8, 128), jnp.int32),
            pltpu.VMEM((sides, 8, 128), jnp.int32),
            pltpu.VMEM((sides + 1, 8, 128), jnp.int32),
            pltpu.SMEM((sides + 1, 8, 128), jnp.int32),
            pltpu.VMEM((2, 2 * own_pairs, reach, lanes), jnp.float32),
            pltpu.VMEM((2, steps, sides, *block), jnp.bfloat16),
            pltpu.VMEM((2, steps, sides, *block), jnp.bfloat16),
            pltpu.VMEM((2, 2, 2, all_pairs * half, lanes), jnp.float32),
            pltpu.VMEM((2, 2, 4, all_pairs * half, lanes), jnp.bfloat16),
            pltpu.VMEM((2, frame_count, 2, *edge), jnp.bfloat16),
            pltpu.VMEM((2, frame_count, 2, *edge), jnp.bfloat16),
            pltpu.SemaphoreType.DMA((sides,)),
            pltpu.SemaphoreType.DMA((2, sides)),
            pltpu.SemaphoreType.DMA((2, 2, sides)),
            pltpu.SemaphoreType.DMA((2, 2)),
            pltpu.SemaphoreType.DMA((2, 2)),
            pltpu.SemaphoreType.DMA((frame_count,)),
        ],
        compiler_params=pltpu.CompilerParams(
            collective_id=0, has_side_effects=True, vmem_limit_bytes=60 * 1024 * 1024
        ),
    )(frames, motion_forward, motion_backward, join_weight, conv_weight)
    outside = pl.BlockSpec(memory_space=pltpu.HBM)
    plain = jax.ShapeDtypeStruct(frames.shape, jnp.bfloat16)
    return pl.pallas_call(
        store_kernel,
        out_shape=(plain, plain),
        in_specs=[pl.BlockSpec(memory_space=pl.ANY)] * 2,
        out_specs=(outside, outside),
        scratch_shapes=[pltpu.SemaphoreType.DMA((2, frame_count))],
        compiler_params=pltpu.CompilerParams(vmem_limit_bytes=4 * 1024 * 1024),
    )(*swept)


def solution(mesh):
    return jax.shard_map(
        on_device,
        mesh=mesh,
        in_specs=(
            P(None, None, ("clips", "tiles"), None),
            P(None, ("clips", "tiles")),
            P(None, ("clips", "tiles")),
            P(),
            P(),
        ),
        out_specs=(
            P(None, None, ("clips", "tiles"), None),
            P(None, None, ("clips", "tiles"), None),
        ),
        check_vma=False,
    )
```

```python
import functools

import jax
import jax.numpy as jnp
from jax import lax
from jax.experimental import pallas as pl
from jax.experimental.pallas import tpu as pltpu
from jax.sharding import PartitionSpec as P

BS = 8
REACH = 2
OFFSETS = tuple(o for o in range(-REACH, REACH + 1) if o != 0)


def leaky(value):
    return jnp.maximum(value, 0.1 * value)


def blockdiag(tile):
    blank = jnp.zeros(tile.shape, tile.dtype)
    return jnp.concatenate(
        [jnp.concatenate([tile, blank], axis=1), jnp.concatenate([blank, tile], axis=1)], axis=0
    )


def matmul_t(left, right):
    return lax.dot_general(
        left, right, (((1,), (1,)), ((), ())), preferred_element_type=jnp.float32
    )


def sweep_kernel(
    dims,
    frames_hbm,
    mf_hbm,
    mb_hbm,
    join_hbm,
    conv_ref,
    ahead_ref,
    behind_ref,
    frames_ref,
    mf_ref,
    mb_ref,
    join_ref,
    conv_v,
    x_ref,
    flip,
    nat,
    wj_ref,
    wc_ref,
    mine,
    theirs,
    table_v,
    table_s,
    cand,
    packed,
    landed,
    h_ref,
    z_ref,
    edge_out,
    edge_in,
    m_send,
    f_send,
    f_recv,
    e_send,
    e_recv,
    x_sem,
):
    frame_count, rows, cols, channels, layers, devices = dims
    outs = (ahead_ref, behind_ref)
    lanes = 2 * channels
    half = cols // 2
    bc = cols // BS
    quad = BS // 2
    own_pairs = rows // 2
    margin = layers // 2
    all_pairs = own_pairs + 2 * margin
    cap = bc // (2 * REACH)
    sides = len(OFFSETS)
    lead = BS
    me = lax.axis_index("tiles")

    def present(offset):
        return (me + offset >= 0) & (me + offset < devices)

    def remote(source, target, send, receive, offset):
        return pltpu.make_async_remote_copy(
            src_ref=source,
            dst_ref=target,
            send_sem=send,
            recv_sem=receive,
            device_id={"tiles": me + offset},
            device_id_type=pl.DeviceIdType.MESH,
        )

    def motion_copy(oi, slot):
        return remote(mine, theirs.at[slot], m_send.at[oi], f_recv.at[1, 1, slot], OFFSETS[oi])

    def feature_copy(d, step, oi, slot, offset):
        return remote(
            packed.at[d, step, oi], landed.at[d, step, slot],
            f_send.at[d, oi], f_recv.at[d, step % 2, slot], offset,
        )

    def edge_copy(d, step, side, slot):
        return remote(
            edge_out.at[d, step, side], edge_in.at[d, step, slot],
            e_send.at[d, side], e_recv.at[d, slot], 1 if side else -1,
        )

    first_frames = sorted({0, frame_count - 1})

    def frame_load(f):
        return pltpu.make_async_copy(frames_hbm.at[f], frames_ref.at[f], x_sem.at[f])

    small_loads = [
        pltpu.make_async_copy(source, target, f_send.at[1, k])
        for k, (source, target) in enumerate(
            [(join_hbm, join_ref), (mf_hbm, mf_ref), (mb_hbm, mb_ref)]
        )
    ]
    weight_load = pltpu.make_async_copy(conv_ref, conv_v, f_send.at[0, 0])
    for f in first_frames:
        frame_load(f).start()
    for load in small_loads:
        load.start()
    weight_load.start()
    for f in range(1, frame_count - 1):
        frame_load(f).start()
    barrier = pltpu.get_barrier_semaphore()
    for offset in OFFSETS:
        @pl.when(present(offset))
        def _():
            pl.semaphore_signal(
                barrier, inc=1, device_id={"tiles": me + offset},
                device_id_type=pl.DeviceIdType.MESH,
            )

    for oi, offset in enumerate(OFFSETS):
        @pl.when(jnp.logical_not(present(offset)))
        def _():
            theirs[oi] = jnp.full(mine.shape, -1, jnp.int32)

    for load in small_loads:
        load.wait()
    mine[...] = jnp.zeros(mine.shape, jnp.int32)
    for step in range(frame_count - 1):
        mine[step:step + 1, 0:bc] = mf_ref[step:step + 1, :]
        back = frame_count - 2 - step
        mine[frame_count - 1 + step:frame_count + step, 0:bc] = mb_ref[back:back + 1, :]

    for d in range(2):
        joined = join_ref[d]
        wj_ref[d, :, :lanes] = blockdiag(joined[:, :channels])
        wj_ref[d, :, lanes:] = blockdiag(joined[:, channels:])

    def load_frame(f):
        frame_load(f).wait()
        flip[0] = frames_ref[f].astype(jnp.float32).reshape(channels * rows, cols)
        parts = jnp.concatenate(
            [flip[0, pl.ds(r, channels, stride=rows), :] for r in range(rows)], axis=0
        ).astype(jnp.bfloat16)
        place = lax.broadcasted_iota(jnp.int32, (cols, cols), 0)
        column = lax.broadcasted_iota(jnp.int32, (cols, cols), 1)
        wanted = jnp.where(place < half, 2 * place, 2 * (place - half) + 1)
        moved = matmul_t((column == wanted).astype(jnp.bfloat16), parts).astype(jnp.bfloat16)
        for parity in range(2):
            for pair in range(own_pairs):
                x_ref[f, parity, pair * half:(pair + 1) * half, :] = moved[
                    parity * half:(parity + 1) * half, pair * lanes:(pair + 1) * lanes
                ]

    def build_weights():
        identity = (
            lax.broadcasted_iota(jnp.int32, (channels, channels), 0)
            == lax.broadcasted_iota(jnp.int32, (channels, channels), 1)
        ).astype(jnp.bfloat16)
        low = lax.broadcasted_iota(jnp.int32, (channels, lanes), 1) < channels

        def build_layer(layer, carry):
            for d in range(2):
                wide = jnp.concatenate(
                    [
                        conv_v[d, layer, 3 * down + across]
                        for across in range(3)
                        for down in (1, 0, 2, 1)
                    ],
                    axis=0,
                )
                turned = matmul_t(identity, wide)
                for across in range(3):
                    at = 2 * across * lanes
                    upper_pair = turned[:, at:at + lanes]
                    lower_pair = turned[:, at + lanes:at + 2 * lanes]
                    blocks = [
                        jnp.where(low, pltpu.roll(upper_pair, channels, axis=1), 0.0),
                        upper_pair,
                        lower_pair,
                        jnp.where(low, 0.0, pltpu.roll(lower_pair, channels, axis=1)),
                    ]
                    for k, block in enumerate(blocks):
                        wc_ref[d, layer, across, k * channels:(k + 1) * channels, :] = block.astype(
                            jnp.bfloat16
                        )
            return carry

        lax.fori_loop(0, layers, build_layer, 0)

    def emit(t):
        identity = (
            lax.broadcasted_iota(jnp.int32, (lanes, lanes), 0)
            == lax.broadcasted_iota(jnp.int32, (lanes, lanes), 1)
        ).astype(jnp.bfloat16)
        for d in range(2):
            for pair in range(own_pairs):
                for parity in range(2):
                    nat[d, pl.ds(pair * cols + parity, half, stride=2), :] = cand[
                        d, 2 * pair + parity, lead:lead + half, :
                    ]
        moved = [matmul_t(identity, nat[d].astype(jnp.bfloat16)) for d in range(2)]
        for d in range(2):
            for pair in range(own_pairs):
                for low in range(2):
                    flip[d, pl.ds(2 * pair + low, channels, stride=rows), :] = moved[d][
                        low * channels:(low + 1) * channels, pair * cols:(pair + 1) * cols
                    ]
        for d in range(2):
            now = t if d == 0 else frame_count - 1 - t
            outs[d][now] = flip[d].reshape(channels, rows, cols).astype(jnp.bfloat16)

    table_load = pltpu.make_async_copy(table_v, table_s, m_send.at[0])

    def build_tables():
        for oi, offset in enumerate(OFFSETS):
            @pl.when(present(offset))
            def _():
                motion_copy(oi, oi).wait_send()
                motion_copy(oi, oi).wait_recv()

        depth = mine.shape[0]
        motion = mine[...]
        local = jnp.concatenate(
            [motion - (me + offset) * bc for offset in OFFSETS]
            + [theirs[oi] - me * bc for oi in range(sides)],
            axis=0,
        )
        lane = lax.broadcasted_iota(jnp.int32, local.shape, 1)
        match = (local >= 0) & (local < bc) & (lane < bc)
        flags = match.astype(jnp.int32)
        total = flags
        shift = 1
        while shift < bc:
            total = total + jnp.where(lane >= shift, pltpu.roll(total, shift, axis=1), 0)
            shift *= 2
        rank = total - flags

        mid = sides * depth
        own = motion - me * bc
        picks = jnp.where((own >= 0) & (own < bc), own, 0)
        for oi in range(sides):
            rows_of = slice(oi * depth, (oi + 1) * depth)
            code = bc + oi * cap + jnp.minimum(rank[rows_of], cap - 1)
            picks = picks + jnp.where(match[rows_of], code, 0)
        table_v[sides] = picks * quad

        wanted, order, chosen = local[mid:], rank[mid:], match[mid:]
        values = jnp.concatenate(
            [jnp.where(chosen & (order == slot), wanted, 0) for slot in range(cap)], axis=0
        )
        shift = 1
        while shift < bc + cap:
            values = values + pltpu.roll(values, shift, axis=1)
            shift *= 2
        place = lax.broadcasted_iota(jnp.int32, (mid, mine.shape[1]), 1)
        gathered = jnp.zeros(place.shape, jnp.int32)
        for slot in range(cap):
            gathered = jnp.where(place == bc + slot, values[slot * mid:(slot + 1) * mid], gathered)
        gathered = gathered * quad
        for oi in range(sides):
            table_v[oi] = gathered[oi * depth:(oi + 1) * depth]
        table_load.start()

    upper = lax.broadcasted_iota(jnp.int32, (BS, lanes), 0) < quad

    def two_blocks(d, k, first, second):
        return jnp.where(
            upper,
            cand[d, k, pl.ds(first + lead, BS), :],
            cand[d, k, pl.ds(second + lead - quad, BS), :],
        )

    def activate(d, slot, start, count, even, odd):
        first = start * half
        size = count * half
        z_ref[d, slot, 1, first:first + size, :] = even.astype(jnp.bfloat16)
        z_ref[d, slot, 2, first:first + size, :] = odd.astype(jnp.bfloat16)
        place = lax.broadcasted_iota(jnp.int32, (count, BS, lanes), 1)
        before = pltpu.roll(odd.reshape(count, half, lanes), 1, axis=1)
        before = jnp.concatenate(
            [jnp.where(place == 0, 0.0, before[:, :BS]), before[:, BS:]], axis=1
        )
        z_ref[d, slot, 0, first:first + size, :] = before.reshape(size, lanes).astype(jnp.bfloat16)
        after = pltpu.roll(even.reshape(count, half, lanes), half - 1, axis=1)
        after = jnp.concatenate(
            [after[:, :half - BS], jnp.where(place == BS - 1, 0.0, after[:, half - BS:])], axis=1
        )
        z_ref[d, slot, 3, first:first + size, :] = after.reshape(size, lanes).astype(jnp.bfloat16)

    def send_edges(d, t, first):
        size = own_pairs * half
        edge = margin * half
        for parity in range(2):
            base = parity * size
            edge_out[d, t, 0, parity] = first[base:base + edge]
            edge_out[d, t, 1, parity] = first[base + size - edge:base + size]
        for side in range(2):
            @pl.when(present(1 if side else -1))
            def _():
                edge_copy(d, t, side, 1 - side).start()
        wide = first.astype(jnp.float32)
        h_ref[d, 0, 0, edge:edge + size, :] = wide[:size]
        h_ref[d, 0, 1, edge:edge + size, :] = wide[size:]
        wide = leaky(wide)
        activate(d, 0, margin, own_pairs, wide[:size], wide[size:])

    def begin_first(d):
        now = 0 if d == 0 else frame_count - 1
        both = jnp.concatenate([x_ref[now, 0], x_ref[now, 1]], axis=0)
        send_edges(d, 0, matmul_t(both, wj_ref[d, :, lanes:]).astype(jnp.bfloat16))

    def begin(d, t):
        step = t - 1
        row = d * (frame_count - 1) + step
        for oi, offset in enumerate(OFFSETS):
            @pl.when(present(offset))
            def _():
                feature_copy(d, step, oi, oi, offset).wait_recv()
                at = lead + (bc + oi * cap) * quad
                for k in range(2 * own_pairs):
                    cand[d, k, at:at + cap * quad, :] = landed[d, step, oi, k].astype(jnp.float32)
        picks = [table_s[sides, row, j] for j in range(bc)]
        now = t if d == 0 else frame_count - 1 - t
        parts = []
        for parity in range(2):
            tiles = [
                two_blocks(d, 2 * pair + parity, picks[2 * j], picks[2 * j + 1])
                for pair in range(own_pairs)
                for j in range(bc // 2)
            ]
            taken = jnp.concatenate(tiles, axis=0).astype(jnp.bfloat16)
            parts.append(jnp.concatenate([taken, x_ref[now, parity]], axis=1))
        both = jnp.concatenate(parts, axis=0)
        send_edges(d, t, matmul_t(both, wj_ref[d]).astype(jnp.bfloat16))
        for oi, offset in enumerate(OFFSETS):
            @pl.when(present(offset))
            def _():
                feature_copy(d, step, oi, oi, offset).wait_send()

    top_inside = (me > 0).astype(jnp.float32)
    bottom_inside = (me < devices - 1).astype(jnp.float32)

    low_lanes = lax.broadcasted_iota(jnp.int32, (1, lanes), 1) < channels
    top_mixed = jnp.where(low_lanes, top_inside, 1.0)
    bottom_mixed = jnp.where(low_lanes, 1.0, bottom_inside)

    def inside(value, layer, begin_pair):
        count = value.shape[0] // half
        pieces = []
        for q in range(count):
            start = 2 * (q + begin_pair) + layer + 1 - layers
            piece = value[q * half:(q + 1) * half]
            if start + 1 < 0:
                piece = piece * top_inside
            elif start < 0:
                piece = piece * top_mixed
            elif start >= rows:
                piece = piece * bottom_inside
            elif start + 1 >= rows:
                piece = piece * bottom_mixed
            pieces.append(piece)
        return jnp.concatenate(pieces, axis=0)

    def multiply(d, layer, spans):
        now = layer
        left = jnp.concatenate(
            [
                jnp.concatenate(
                    [
                        z_ref[d, now, k, (first + low) * half:(last + low) * half, :]
                        for k in range(4)
                        for low in range(2)
                    ],
                    axis=1,
                )
                for first, last in spans
            ],
            axis=0,
        )
        taps = [wc_ref[d, layer, across] for across in range(3)]
        blank = jnp.zeros(taps[0].shape, jnp.bfloat16)
        right = jnp.concatenate(
            [
                jnp.concatenate([taps[0], blank], axis=1),
                jnp.concatenate([taps[1], taps[0]], axis=1),
                jnp.concatenate([taps[2], taps[1]], axis=1),
                jnp.concatenate([blank, taps[2]], axis=1),
            ],
            axis=0,
        )
        summed = jnp.dot(left, right, preferred_element_type=jnp.float32)
        parts, at = [], 0
        for first, last in spans:
            parts.append(summed[at:at + (last - first) * half])
            at += (last - first) * half
        return parts

    def run(d, jobs, ahead):
        pending = [multiply(d, *jobs[0])]
        for k, (layer, spans) in enumerate(jobs):
            if k + 1 < len(jobs) and ahead:
                pending.append(multiply(d, *jobs[k + 1]))
            for span, summed in zip(spans, pending[k]):
                settle(d, layer, *span, summed)
            if k + 1 < len(jobs) and not ahead:
                pending.append(multiply(d, *jobs[k + 1]))

    def inner_end(layer):
        return all_pairs - margin - 1 - layer

    def inner(d):
        jobs = [(layer, [(margin, inner_end(layer))]) for layer in range(layers)]
        run(d, [job for job in jobs if job[1][0][1] > margin], False)

    def settle(d, layer, first, last, summed):
        now, later = layer, layer + 1
        count = last - first
        base = first * half
        size = count * half
        first_half = lax.broadcasted_iota(jnp.int32, (size, lanes), 1) < channels
        fresh = []
        for parity in range(2):
            kept = jnp.where(
                first_half,
                h_ref[d, now, parity, base + half:base + half + size, :],
                h_ref[d, now, parity, base:base + size, :],
            )
            fresh.append(
                pltpu.roll(kept, channels, axis=1) + summed[:, parity * lanes:(parity + 1) * lanes]
            )
        if layer < layers - 1:
            for parity in range(2):
                h_ref[d, later, parity, base:base + size, :] = fresh[parity]
            activate(
                d, later, first, count,
                inside(leaky(fresh[0]), layer, first), inside(leaky(fresh[1]), layer, first),
            )
        else:
            for parity in range(2):
                rounded = fresh[parity].astype(jnp.bfloat16).astype(jnp.float32)
                for pair in range(first, last):
                    at = (pair - first) * half
                    cand[d, 2 * pair + parity, lead:lead + half, :] = rounded[at:at + half]

    def finish(d, t):
        edge = margin * half
        for side in range(2):
            pair = side * (margin + own_pairs)
            start = pair * half

            @pl.when(present(1 if side else -1))
            def _():
                edge_copy(d, t, side, side).wait_recv()
                even = edge_in[d, t, side, 0].astype(jnp.float32)
                odd = edge_in[d, t, side, 1].astype(jnp.float32)
                h_ref[d, 0, 0, start:start + edge, :] = even
                h_ref[d, 0, 1, start:start + edge, :] = odd
                activate(d, 0, pair, margin, leaky(even), leaky(odd))

            @pl.when(jnp.logical_not(present(1 if side else -1)))
            def _():
                for parity in range(2):
                    h_ref[d, 0, parity, start:start + edge, :] = jnp.zeros((edge, lanes), jnp.float32)
                for k in range(4):
                    z_ref[d, 0, k, start:start + edge, :] = jnp.zeros((edge, lanes), jnp.bfloat16)

        jobs = []
        for layer in range(layers):
            top = (0, margin)
            bottom = (max(margin, inner_end(layer)), all_pairs - 1 - layer)
            jobs += [(layer, [top]), (layer, [bottom])]
        run(d, jobs, True)

        if d == 0:
            @pl.when(t == 0)
            def _():
                table_load.wait()

        @pl.when(t < frame_count - 1)
        def _():
            row = d * (frame_count - 1) + t
            flag = (me // 2) % 2
            for k in range(sides):
                oi = k + flag * (sides - 1 - 2 * k)
                offset = oi - REACH + (oi + REACH) // (2 * REACH)
                picks = [table_s[oi, row, bc + slot] for slot in range(cap)]
                for tile in range(2 * own_pairs):
                    packed[d, t, oi, tile] = jnp.concatenate(
                        [
                            two_blocks(d, tile, picks[slot], picks[slot + 1])
                            for slot in range(0, cap, 2)
                        ],
                        axis=0,
                    ).astype(jnp.bfloat16)

                @pl.when(present(offset))
                def _():
                    feature_copy(d, t, oi, sides - 1 - oi, offset).start()

        for side in range(2):
            @pl.when(present(1 if side else -1))
            def _():
                edge_copy(d, t, side, side).wait_send()

    for f in first_frames:
        load_frame(f)

    peers = jnp.minimum(me, REACH) + jnp.minimum(devices - 1 - me, REACH)
    pl.semaphore_wait(barrier, peers)

    for oi, offset in enumerate(OFFSETS):
        @pl.when(present(offset))
        def _():
            motion_copy(oi, sides - 1 - oi).start()
    for d in range(2):
        begin_first(d)

    def load_rest(f, carry):
        load_frame(f)
        return carry

    weight_load.wait()
    build_weights()
    inner(0)
    build_tables()

    def frame_step(t, carry):
        finish(0, t)
        inner(1)
        finish(1, t)

        @pl.when(t == 0)
        def _():
            lax.fori_loop(1, frame_count - 1, load_rest, 0)

        emit(t)

        @pl.when(t < frame_count - 1)
        def _():
            begin(0, t + 1)
            inner(0)
            begin(1, t + 1)

        return carry

    lax.fori_loop(0, frame_count, frame_step, 0)


def store_kernel(ahead_ref, behind_ref, ahead_out, behind_out, sems):
    copies = [
        pltpu.make_async_copy(source.at[f], target.at[f], sems.at[k, f])
        for k, (source, target) in enumerate([(ahead_ref, ahead_out), (behind_ref, behind_out)])
        for f in range(source.shape[0])
    ]
    for copy in copies:
        copy.start()
    for copy in copies:
        copy.wait()


def on_device(frames, motion_forward, motion_backward, join_weight, conv_weight):
    frame_count, channels, rows, cols = frames.shape
    layers = conv_weight.shape[1]
    devices = lax.axis_size("tiles")
    lanes = 2 * channels
    half = cols // 2
    bc = rows // BS * (cols // BS)
    cap = bc // (2 * REACH)
    sides = len(OFFSETS)
    steps = frame_count - 1
    own_pairs = rows // 2
    margin = layers // 2
    all_pairs = own_pairs + 2 * margin
    quad = BS // 2
    reach = 2 * BS + (bc + sides * cap) * quad

    dims = (frame_count, rows, cols, channels, layers, devices)
    vmem = pl.BlockSpec(memory_space=pltpu.VMEM)
    result = pltpu.VMEM(frames.shape, jnp.bfloat16)
    block = (2 * own_pairs, cap * quad, lanes)
    edge = (2, margin * half, lanes)
    swept = pl.pallas_call(
        functools.partial(sweep_kernel, dims),
        out_shape=(result, result),
        in_specs=[pl.BlockSpec(memory_space=pltpu.HBM)] * 5,
        out_specs=(vmem, vmem),
        scratch_shapes=[
            pltpu.VMEM(frames.shape, jnp.bfloat16),
            pltpu.VMEM(motion_forward.shape, jnp.int32),
            pltpu.VMEM(motion_backward.shape, jnp.int32),
            pltpu.VMEM(join_weight.shape, jnp.bfloat16),
            pltpu.VMEM(conv_weight.shape, jnp.bfloat16),
            pltpu.VMEM((frame_count, 2, own_pairs * half, lanes), jnp.bfloat16),
            pltpu.VMEM((2, channels * rows, cols), jnp.float32),
            pltpu.VMEM((2, own_pairs * cols, lanes), jnp.float32),
            pltpu.VMEM((2, lanes, 2 * lanes), jnp.bfloat16),
            pltpu.VMEM((2, layers, 3, 2 * lanes, lanes), jnp.bfloat16),
            pltpu.VMEM((8, 128), jnp.int32),
            pltpu.VMEM((sides, 8, 128), jnp.int32),
            pltpu.VMEM((sides + 1, 8, 128), jnp.int32),
            pltpu.SMEM((sides + 1, 8, 128), jnp.int32),
            pltpu.VMEM((2, 2 * own_pairs, reach, lanes), jnp.float32),
            pltpu.VMEM((2, steps, sides, *block), jnp.bfloat16),
            pltpu.VMEM((2, steps, sides, *block), jnp.bfloat16),
            pltpu.VMEM((2, layers, 2, all_pairs * half, lanes), jnp.float32),
            pltpu.VMEM((2, layers, 4, all_pairs * half, lanes), jnp.bfloat16),
            pltpu.VMEM((2, frame_count, 2, *edge), jnp.bfloat16),
            pltpu.VMEM((2, frame_count, 2, *edge), jnp.bfloat16),
            pltpu.SemaphoreType.DMA((sides,)),
            pltpu.SemaphoreType.DMA((2, sides)),
            pltpu.SemaphoreType.DMA((2, 2, sides)),
            pltpu.SemaphoreType.DMA((2, 2)),
            pltpu.SemaphoreType.DMA((2, 2)),
            pltpu.SemaphoreType.DMA((frame_count,)),
        ],
        compiler_params=pltpu.CompilerParams(
            collective_id=0, has_side_effects=True, vmem_limit_bytes=60 * 1024 * 1024
        ),
    )(frames, motion_forward, motion_backward, join_weight, conv_weight)
    outside = pl.BlockSpec(memory_space=pltpu.HBM)
    plain = jax.ShapeDtypeStruct(frames.shape, jnp.bfloat16)
    return pl.pallas_call(
        store_kernel,
        out_shape=(plain, plain),
        in_specs=[pl.BlockSpec(memory_space=pl.ANY)] * 2,
        out_specs=(outside, outside),
        scratch_shapes=[pltpu.SemaphoreType.DMA((2, frame_count))],
        compiler_params=pltpu.CompilerParams(vmem_limit_bytes=4 * 1024 * 1024),
    )(*swept)


def solution(mesh):
    return jax.shard_map(
        on_device,
        mesh=mesh,
        in_specs=(
            P(None, None, ("clips", "tiles"), None),
            P(None, ("clips", "tiles")),
            P(None, ("clips", "tiles")),
            P(),
            P(),
        ),
        out_specs=(
            P(None, None, ("clips", "tiles"), None),
            P(None, None, ("clips", "tiles"), None),
        ),
        check_vma=False,
    )
```

```python
import functools

import jax
import jax.numpy as jnp
from jax import lax
from jax.experimental import pallas as pl
from jax.experimental.pallas import tpu as pltpu
from jax.sharding import PartitionSpec as P

BS = 8
REACH = 2
OFFSETS = tuple(o for o in range(-REACH, REACH + 1) if o != 0)


def leaky(value):
    return jnp.maximum(value, 0.1 * value)


def blockdiag(tile):
    blank = jnp.zeros(tile.shape, tile.dtype)
    return jnp.concatenate(
        [jnp.concatenate([tile, blank], axis=1), jnp.concatenate([blank, tile], axis=1)], axis=0
    )


def matmul_t(left, right):
    return lax.dot_general(
        left, right, (((1,), (1,)), ((), ())), preferred_element_type=jnp.float32
    )


def sweep_kernel(
    dims,
    frames_hbm,
    mf_hbm,
    mb_hbm,
    join_hbm,
    conv_ref,
    ahead_ref,
    behind_ref,
    frames_ref,
    mf_ref,
    mb_ref,
    join_ref,
    conv_v,
    x_ref,
    flip,
    nat,
    wj_ref,
    wc_ref,
    mine,
    theirs,
    table_v,
    table_s,
    cand,
    packed,
    landed,
    h_ref,
    z_ref,
    edge_out,
    edge_in,
    m_send,
    f_send,
    f_recv,
    e_send,
    e_recv,
    x_sem,
):
    frame_count, rows, cols, channels, layers, devices = dims
    outs = (ahead_ref, behind_ref)
    lanes = 2 * channels
    half = cols // 2
    bc = cols // BS
    quad = BS // 2
    own_pairs = rows // 2
    margin = layers // 2
    all_pairs = own_pairs + 2 * margin
    cap = bc // (2 * REACH)
    sides = len(OFFSETS)
    lead = BS
    me = lax.axis_index("tiles")

    def present(offset):
        return (me + offset >= 0) & (me + offset < devices)

    def remote(source, target, send, receive, offset):
        return pltpu.make_async_remote_copy(
            src_ref=source,
            dst_ref=target,
            send_sem=send,
            recv_sem=receive,
            device_id={"tiles": me + offset},
            device_id_type=pl.DeviceIdType.MESH,
        )

    def motion_copy(oi, slot):
        return remote(mine, theirs.at[slot], m_send.at[oi], f_recv.at[1, 1, slot], OFFSETS[oi])

    def feature_copy(d, step, oi, slot, offset):
        return remote(
            packed.at[d, step, oi], landed.at[d, step, slot],
            f_send.at[d, oi], f_recv.at[d, step % 2, slot], offset,
        )

    def edge_copy(d, step, side, slot):
        return remote(
            edge_out.at[d, step, side], edge_in.at[d, step, slot],
            e_send.at[d, side], e_recv.at[d, slot], 1 if side else -1,
        )

    first_frames = sorted({0, frame_count - 1})

    def frame_load(f):
        return pltpu.make_async_copy(frames_hbm.at[f], frames_ref.at[f], x_sem.at[f])

    small_loads = [
        pltpu.make_async_copy(source, target, f_send.at[1, k])
        for k, (source, target) in enumerate(
            [(join_hbm, join_ref), (mf_hbm, mf_ref), (mb_hbm, mb_ref)]
        )
    ]
    weight_load = pltpu.make_async_copy(conv_ref, conv_v, f_send.at[0, 0])
    for f in first_frames:
        frame_load(f).start()
    for load in small_loads:
        load.start()
    weight_load.start()
    for f in range(1, frame_count - 1):
        frame_load(f).start()
    barrier = pltpu.get_barrier_semaphore()
    for offset in OFFSETS:
        @pl.when(present(offset))
        def _():
            pl.semaphore_signal(
                barrier, inc=1, device_id={"tiles": me + offset},
                device_id_type=pl.DeviceIdType.MESH,
            )

    for oi, offset in enumerate(OFFSETS):
        @pl.when(jnp.logical_not(present(offset)))
        def _():
            theirs[oi] = jnp.full(mine.shape, -1, jnp.int32)

    for load in small_loads:
        load.wait()
    mine[...] = jnp.zeros(mine.shape, jnp.int32)
    for step in range(frame_count - 1):
        mine[step:step + 1, 0:bc] = mf_ref[step:step + 1, :]
        back = frame_count - 2 - step
        mine[frame_count - 1 + step:frame_count + step, 0:bc] = mb_ref[back:back + 1, :]

    for d in range(2):
        joined = join_ref[d]
        wj_ref[d, :, :lanes] = blockdiag(joined[:, :channels])
        wj_ref[d, :, lanes:] = blockdiag(joined[:, channels:])

    def load_frame(f):
        frame_load(f).wait()
        flip[0] = frames_ref[f].astype(jnp.float32).reshape(channels * rows, cols)
        parts = jnp.concatenate(
            [flip[0, pl.ds(r, channels, stride=rows), :] for r in range(rows)], axis=0
        ).astype(jnp.bfloat16)
        place = lax.broadcasted_iota(jnp.int32, (cols, cols), 0)
        column = lax.broadcasted_iota(jnp.int32, (cols, cols), 1)
        wanted = jnp.where(place < half, 2 * place, 2 * (place - half) + 1)
        moved = matmul_t((column == wanted).astype(jnp.bfloat16), parts).astype(jnp.bfloat16)
        for parity in range(2):
            for pair in range(own_pairs):
                x_ref[f, parity, pair * half:(pair + 1) * half, :] = moved[
                    parity * half:(parity + 1) * half, pair * lanes:(pair + 1) * lanes
                ]

    def build_weights():
        identity = (
            lax.broadcasted_iota(jnp.int32, (channels, channels), 0)
            == lax.broadcasted_iota(jnp.int32, (channels, channels), 1)
        ).astype(jnp.bfloat16)
        low = lax.broadcasted_iota(jnp.int32, (channels, lanes), 1) < channels

        def build_layer(layer, carry):
            for d in range(2):
                wide = jnp.concatenate(
                    [
                        conv_v[d, layer, 3 * down + across]
                        for across in range(3)
                        for down in (1, 0, 2, 1)
                    ],
                    axis=0,
                )
                turned = matmul_t(identity, wide)
                for across in range(3):
                    at = 2 * across * lanes
                    upper_pair = turned[:, at:at + lanes]
                    lower_pair = turned[:, at + lanes:at + 2 * lanes]
                    blocks = [
                        jnp.where(low, pltpu.roll(upper_pair, channels, axis=1), 0.0),
                        upper_pair,
                        lower_pair,
                        jnp.where(low, 0.0, pltpu.roll(lower_pair, channels, axis=1)),
                    ]
                    for k, block in enumerate(blocks):
                        wc_ref[d, layer, across, k * channels:(k + 1) * channels, :] = block.astype(
                            jnp.bfloat16
                        )
            return carry

        lax.fori_loop(0, layers, build_layer, 0)

    def emit(t):
        identity = (
            lax.broadcasted_iota(jnp.int32, (lanes, lanes), 0)
            == lax.broadcasted_iota(jnp.int32, (lanes, lanes), 1)
        ).astype(jnp.bfloat16)
        for d in range(2):
            for pair in range(own_pairs):
                for parity in range(2):
                    nat[d, pl.ds(pair * cols + parity, half, stride=2), :] = cand[
                        d, 2 * pair + parity, lead:lead + half, :
                    ]
        moved = [matmul_t(identity, nat[d].astype(jnp.bfloat16)) for d in range(2)]
        for d in range(2):
            for pair in range(own_pairs):
                for low in range(2):
                    flip[d, pl.ds(2 * pair + low, channels, stride=rows), :] = moved[d][
                        low * channels:(low + 1) * channels, pair * cols:(pair + 1) * cols
                    ]
        for d in range(2):
            now = t if d == 0 else frame_count - 1 - t
            outs[d][now] = flip[d].reshape(channels, rows, cols).astype(jnp.bfloat16)

    table_load = pltpu.make_async_copy(table_v, table_s, m_send.at[0])

    def build_tables():
        for oi, offset in enumerate(OFFSETS):
            @pl.when(present(offset))
            def _():
                motion_copy(oi, oi).wait_send()
                motion_copy(oi, oi).wait_recv()

        depth = mine.shape[0]
        motion = mine[...]
        local = jnp.concatenate(
            [motion - (me + offset) * bc for offset in OFFSETS]
            + [theirs[oi] - me * bc for oi in range(sides)],
            axis=0,
        )
        lane = lax.broadcasted_iota(jnp.int32, local.shape, 1)
        match = (local >= 0) & (local < bc) & (lane < bc)
        flags = match.astype(jnp.int32)
        total = flags
        shift = 1
        while shift < bc:
            total = total + jnp.where(lane >= shift, pltpu.roll(total, shift, axis=1), 0)
            shift *= 2
        rank = total - flags

        mid = sides * depth
        own = motion - me * bc
        picks = jnp.where((own >= 0) & (own < bc), own, 0)
        for oi in range(sides):
            rows_of = slice(oi * depth, (oi + 1) * depth)
            code = bc + oi * cap + jnp.minimum(rank[rows_of], cap - 1)
            picks = picks + jnp.where(match[rows_of], code, 0)
        table_v[sides] = picks * quad

        wanted, order, chosen = local[mid:], rank[mid:], match[mid:]
        values = jnp.concatenate(
            [jnp.where(chosen & (order == slot), wanted, 0) for slot in range(cap)], axis=0
        )
        shift = 1
        while shift < bc + cap:
            values = values + pltpu.roll(values, shift, axis=1)
            shift *= 2
        place = lax.broadcasted_iota(jnp.int32, (mid, mine.shape[1]), 1)
        gathered = jnp.zeros(place.shape, jnp.int32)
        for slot in range(cap):
            gathered = jnp.where(place == bc + slot, values[slot * mid:(slot + 1) * mid], gathered)
        gathered = gathered * quad
        for oi in range(sides):
            table_v[oi] = gathered[oi * depth:(oi + 1) * depth]
        table_load.start()

    upper = lax.broadcasted_iota(jnp.int32, (BS, lanes), 0) < quad

    def two_blocks(d, k, first, second):
        return jnp.where(
            upper,
            cand[d, k, pl.ds(first + lead, BS), :],
            cand[d, k, pl.ds(second + lead - quad, BS), :],
        )

    def activate(d, slot, start, count, even, odd):
        first = start * half
        size = count * half
        z_ref[d, slot, 1, first:first + size, :] = even.astype(jnp.bfloat16)
        z_ref[d, slot, 2, first:first + size, :] = odd.astype(jnp.bfloat16)
        place = lax.broadcasted_iota(jnp.int32, (count, BS, lanes), 1)
        before = pltpu.roll(odd.reshape(count, half, lanes), 1, axis=1)
        before = jnp.concatenate(
            [jnp.where(place == 0, 0.0, before[:, :BS]), before[:, BS:]], axis=1
        )
        z_ref[d, slot, 0, first:first + size, :] = before.reshape(size, lanes).astype(jnp.bfloat16)
        after = pltpu.roll(even.reshape(count, half, lanes), half - 1, axis=1)
        after = jnp.concatenate(
            [after[:, :half - BS], jnp.where(place == BS - 1, 0.0, after[:, half - BS:])], axis=1
        )
        z_ref[d, slot, 3, first:first + size, :] = after.reshape(size, lanes).astype(jnp.bfloat16)

    def send_edges(d, t, first):
        size = own_pairs * half
        edge = margin * half
        for parity in range(2):
            base = parity * size
            edge_out[d, t, 0, parity] = first[base:base + edge]
            edge_out[d, t, 1, parity] = first[base + size - edge:base + size]
        for side in range(2):
            @pl.when(present(1 if side else -1))
            def _():
                edge_copy(d, t, side, 1 - side).start()
        wide = first.astype(jnp.float32)
        h_ref[d, 0, 0, edge:edge + size, :] = wide[:size]
        h_ref[d, 0, 1, edge:edge + size, :] = wide[size:]
        wide = leaky(wide)
        activate(d, 0, margin, own_pairs, wide[:size], wide[size:])

    def begin_first(d):
        now = 0 if d == 0 else frame_count - 1
        both = jnp.concatenate([x_ref[now, 0], x_ref[now, 1]], axis=0)
        send_edges(d, 0, matmul_t(both, wj_ref[d, :, lanes:]).astype(jnp.bfloat16))

    def begin(d, t):
        step = t - 1
        row = d * (frame_count - 1) + step
        for oi, offset in enumerate(OFFSETS):
            @pl.when(present(offset))
            def _():
                feature_copy(d, step, oi, oi, offset).wait_recv()
                at = lead + (bc + oi * cap) * quad
                for k in range(2 * own_pairs):
                    cand[d, k, at:at + cap * quad, :] = landed[d, step, oi, k].astype(jnp.float32)
        picks = [table_s[sides, row, j] for j in range(bc)]
        now = t if d == 0 else frame_count - 1 - t
        parts = []
        for parity in range(2):
            tiles = [
                two_blocks(d, 2 * pair + parity, picks[2 * j], picks[2 * j + 1])
                for pair in range(own_pairs)
                for j in range(bc // 2)
            ]
            taken = jnp.concatenate(tiles, axis=0).astype(jnp.bfloat16)
            parts.append(jnp.concatenate([taken, x_ref[now, parity]], axis=1))
        both = jnp.concatenate(parts, axis=0)
        send_edges(d, t, matmul_t(both, wj_ref[d]).astype(jnp.bfloat16))
        for oi, offset in enumerate(OFFSETS):
            @pl.when(present(offset))
            def _():
                feature_copy(d, step, oi, oi, offset).wait_send()

    top_inside = (me > 0).astype(jnp.float32)
    bottom_inside = (me < devices - 1).astype(jnp.float32)

    low_lanes = lax.broadcasted_iota(jnp.int32, (1, lanes), 1) < channels
    top_mixed = jnp.where(low_lanes, top_inside, 1.0)
    bottom_mixed = jnp.where(low_lanes, 1.0, bottom_inside)

    def inside(value, layer, begin_pair):
        count = value.shape[0] // half
        pieces = []
        for q in range(count):
            start = 2 * (q + begin_pair) + layer + 1 - layers
            piece = value[q * half:(q + 1) * half]
            if start + 1 < 0:
                piece = piece * top_inside
            elif start < 0:
                piece = piece * top_mixed
            elif start >= rows:
                piece = piece * bottom_inside
            elif start + 1 >= rows:
                piece = piece * bottom_mixed
            pieces.append(piece)
        return jnp.concatenate(pieces, axis=0)

    def multiply(d, layer, spans):
        now = layer
        left = jnp.concatenate(
            [
                jnp.concatenate(
                    [
                        z_ref[d, now, k, (first + low) * half:(last + low) * half, :]
                        for k in range(4)
                        for low in range(2)
                    ],
                    axis=1,
                )
                for first, last in spans
            ],
            axis=0,
        )
        taps = [wc_ref[d, layer, across] for across in range(3)]
        blank = jnp.zeros(taps[0].shape, jnp.bfloat16)
        right = jnp.concatenate(
            [
                jnp.concatenate([taps[0], blank], axis=1),
                jnp.concatenate([taps[1], taps[0]], axis=1),
                jnp.concatenate([taps[2], taps[1]], axis=1),
                jnp.concatenate([blank, taps[2]], axis=1),
            ],
            axis=0,
        )
        summed = jnp.dot(left, right, preferred_element_type=jnp.float32)
        parts, at = [], 0
        for first, last in spans:
            parts.append(summed[at:at + (last - first) * half])
            at += (last - first) * half
        return parts

    def run(d, jobs, ahead):
        pending = [multiply(d, *jobs[0])]
        for k, (layer, spans) in enumerate(jobs):
            if k + 1 < len(jobs) and ahead:
                pending.append(multiply(d, *jobs[k + 1]))
            for span, summed in zip(spans, pending[k]):
                settle(d, layer, *span, summed)
            if k + 1 < len(jobs) and not ahead:
                pending.append(multiply(d, *jobs[k + 1]))

    def inner_end(layer):
        return all_pairs - margin - 1 - layer

    def inner(d):
        jobs = [(layer, [(margin, inner_end(layer))]) for layer in range(layers)]
        run(d, [job for job in jobs if job[1][0][1] > margin], False)

    def settle(d, layer, first, last, summed):
        now, later = layer, layer + 1
        count = last - first
        base = first * half
        size = count * half
        first_half = lax.broadcasted_iota(jnp.int32, (size, lanes), 1) < channels
        fresh = []
        for parity in range(2):
            kept = jnp.where(
                first_half,
                h_ref[d, now, parity, base + half:base + half + size, :],
                h_ref[d, now, parity, base:base + size, :],
            )
            fresh.append(
                pltpu.roll(kept, channels, axis=1) + summed[:, parity * lanes:(parity + 1) * lanes]
            )
        if layer < layers - 1:
            for parity in range(2):
                h_ref[d, later, parity, base:base + size, :] = fresh[parity]
            activate(
                d, later, first, count,
                inside(leaky(fresh[0]), layer, first), inside(leaky(fresh[1]), layer, first),
            )
        else:
            for parity in range(2):
                rounded = fresh[parity].astype(jnp.bfloat16).astype(jnp.float32)
                for pair in range(first, last):
                    at = (pair - first) * half
                    cand[d, 2 * pair + parity, lead:lead + half, :] = rounded[at:at + half]

    def send_last(d, t):
        flag = (me // 2) % 2
        oi = (sides - 1) * (1 - flag)
        offset = oi - REACH + (oi + REACH) // (2 * REACH)

        @pl.when(present(offset) & (t < frame_count - 1))
        def _():
            feature_copy(d, t, oi, sides - 1 - oi, offset).start()

    def finish(d, t):
        edge = margin * half
        for side in range(2):
            pair = side * (margin + own_pairs)
            start = pair * half

            @pl.when(present(1 if side else -1))
            def _():
                edge_copy(d, t, side, side).wait_recv()
                even = edge_in[d, t, side, 0].astype(jnp.float32)
                odd = edge_in[d, t, side, 1].astype(jnp.float32)
                h_ref[d, 0, 0, start:start + edge, :] = even
                h_ref[d, 0, 1, start:start + edge, :] = odd
                activate(d, 0, pair, margin, leaky(even), leaky(odd))

            @pl.when(jnp.logical_not(present(1 if side else -1)))
            def _():
                for parity in range(2):
                    h_ref[d, 0, parity, start:start + edge, :] = jnp.zeros((edge, lanes), jnp.float32)
                for k in range(4):
                    z_ref[d, 0, k, start:start + edge, :] = jnp.zeros((edge, lanes), jnp.bfloat16)

        jobs = []
        for layer in range(layers):
            top = (0, margin)
            bottom = (max(margin, inner_end(layer)), all_pairs - 1 - layer)
            jobs += [(layer, [top]), (layer, [bottom])]
        run(d, jobs, True)

        if d == 0:
            @pl.when(t == 0)
            def _():
                table_load.wait()

        @pl.when(t < frame_count - 1)
        def _():
            row = d * (frame_count - 1) + t
            flag = (me // 2) % 2
            for k in range(sides):
                oi = k + flag * (sides - 1 - 2 * k)
                offset = oi - REACH + (oi + REACH) // (2 * REACH)
                picks = [table_s[oi, row, bc + slot] for slot in range(cap)]
                for tile in range(2 * own_pairs):
                    packed[d, t, oi, tile] = jnp.concatenate(
                        [
                            two_blocks(d, tile, picks[slot], picks[slot + 1])
                            for slot in range(0, cap, 2)
                        ],
                        axis=0,
                    ).astype(jnp.bfloat16)

                if k < sides - 1:
                    @pl.when(present(offset))
                    def _():
                        feature_copy(d, t, oi, sides - 1 - oi, offset).start()

        for side in range(2):
            @pl.when(present(1 if side else -1))
            def _():
                edge_copy(d, t, side, side).wait_send()

    for f in first_frames:
        load_frame(f)

    peers = jnp.minimum(me, REACH) + jnp.minimum(devices - 1 - me, REACH)
    pl.semaphore_wait(barrier, peers)

    for oi, offset in enumerate(OFFSETS):
        @pl.when(present(offset))
        def _():
            motion_copy(oi, sides - 1 - oi).start()
    for d in range(2):
        begin_first(d)

    def load_rest(f, carry):
        load_frame(f)
        return carry

    weight_load.wait()
    build_weights()
    inner(0)
    build_tables()

    def frame_step(t, carry):
        finish(0, t)
        inner(1)
        send_last(0, t)
        finish(1, t)

        @pl.when(t == 0)
        def _():
            lax.fori_loop(1, frame_count - 1, load_rest, 0)

        emit(t)
        send_last(1, t)

        @pl.when(t < frame_count - 1)
        def _():
            begin(0, t + 1)
            inner(0)
            begin(1, t + 1)

        return carry

    lax.fori_loop(0, frame_count, frame_step, 0)


def store_kernel(ahead_ref, behind_ref, ahead_out, behind_out, sems):
    copies = [
        pltpu.make_async_copy(source.at[f], target.at[f], sems.at[k, f])
        for k, (source, target) in enumerate([(ahead_ref, ahead_out), (behind_ref, behind_out)])
        for f in range(source.shape[0])
    ]
    for copy in copies:
        copy.start()
    for copy in copies:
        copy.wait()


def on_device(frames, motion_forward, motion_backward, join_weight, conv_weight):
    frame_count, channels, rows, cols = frames.shape
    layers = conv_weight.shape[1]
    devices = lax.axis_size("tiles")
    lanes = 2 * channels
    half = cols // 2
    bc = rows // BS * (cols // BS)
    cap = bc // (2 * REACH)
    sides = len(OFFSETS)
    steps = frame_count - 1
    own_pairs = rows // 2
    margin = layers // 2
    all_pairs = own_pairs + 2 * margin
    quad = BS // 2
    reach = 2 * BS + (bc + sides * cap) * quad

    dims = (frame_count, rows, cols, channels, layers, devices)
    vmem = pl.BlockSpec(memory_space=pltpu.VMEM)
    result = pltpu.VMEM(frames.shape, jnp.bfloat16)
    block = (2 * own_pairs, cap * quad, lanes)
    edge = (2, margin * half, lanes)
    swept = pl.pallas_call(
        functools.partial(sweep_kernel, dims),
        out_shape=(result, result),
        in_specs=[pl.BlockSpec(memory_space=pltpu.HBM)] * 5,
        out_specs=(vmem, vmem),
        scratch_shapes=[
            pltpu.VMEM(frames.shape, jnp.bfloat16),
            pltpu.VMEM(motion_forward.shape, jnp.int32),
            pltpu.VMEM(motion_backward.shape, jnp.int32),
            pltpu.VMEM(join_weight.shape, jnp.bfloat16),
            pltpu.VMEM(conv_weight.shape, jnp.bfloat16),
            pltpu.VMEM((frame_count, 2, own_pairs * half, lanes), jnp.bfloat16),
            pltpu.VMEM((2, channels * rows, cols), jnp.float32),
            pltpu.VMEM((2, own_pairs * cols, lanes), jnp.float32),
            pltpu.VMEM((2, lanes, 2 * lanes), jnp.bfloat16),
            pltpu.VMEM((2, layers, 3, 2 * lanes, lanes), jnp.bfloat16),
            pltpu.VMEM((8, 128), jnp.int32),
            pltpu.VMEM((sides, 8, 128), jnp.int32),
            pltpu.VMEM((sides + 1, 8, 128), jnp.int32),
            pltpu.SMEM((sides + 1, 8, 128), jnp.int32),
            pltpu.VMEM((2, 2 * own_pairs, reach, lanes), jnp.float32),
            pltpu.VMEM((2, steps, sides, *block), jnp.bfloat16),
            pltpu.VMEM((2, steps, sides, *block), jnp.bfloat16),
            pltpu.VMEM((2, layers, 2, all_pairs * half, lanes), jnp.float32),
            pltpu.VMEM((2, layers, 4, all_pairs * half, lanes), jnp.bfloat16),
            pltpu.VMEM((2, frame_count, 2, *edge), jnp.bfloat16),
            pltpu.VMEM((2, frame_count, 2, *edge), jnp.bfloat16),
            pltpu.SemaphoreType.DMA((sides,)),
            pltpu.SemaphoreType.DMA((2, sides)),
            pltpu.SemaphoreType.DMA((2, 2, sides)),
            pltpu.SemaphoreType.DMA((2, 2)),
            pltpu.SemaphoreType.DMA((2, 2)),
            pltpu.SemaphoreType.DMA((frame_count,)),
        ],
        compiler_params=pltpu.CompilerParams(
            collective_id=0, has_side_effects=True, vmem_limit_bytes=60 * 1024 * 1024
        ),
    )(frames, motion_forward, motion_backward, join_weight, conv_weight)
    outside = pl.BlockSpec(memory_space=pltpu.HBM)
    plain = jax.ShapeDtypeStruct(frames.shape, jnp.bfloat16)
    return pl.pallas_call(
        store_kernel,
        out_shape=(plain, plain),
        in_specs=[pl.BlockSpec(memory_space=pl.ANY)] * 2,
        out_specs=(outside, outside),
        scratch_shapes=[pltpu.SemaphoreType.DMA((2, frame_count))],
        compiler_params=pltpu.CompilerParams(vmem_limit_bytes=4 * 1024 * 1024),
    )(*swept)


def solution(mesh):
    return jax.shard_map(
        on_device,
        mesh=mesh,
        in_specs=(
            P(None, None, ("clips", "tiles"), None),
            P(None, ("clips", "tiles")),
            P(None, ("clips", "tiles")),
            P(),
            P(),
        ),
        out_specs=(
            P(None, None, ("clips", "tiles"), None),
            P(None, None, ("clips", "tiles"), None),
        ),
        check_vma=False,
    )
```

```python
import functools

import jax
import jax.numpy as jnp
from jax import lax
from jax.experimental import pallas as pl
from jax.experimental.pallas import tpu as pltpu
from jax.sharding import PartitionSpec as P

BS = 8
REACH = 2
OFFSETS = tuple(o for o in range(-REACH, REACH + 1) if o != 0)


def leaky(value):
    return jnp.maximum(value, 0.1 * value)


def blockdiag(tile):
    blank = jnp.zeros(tile.shape, tile.dtype)
    return jnp.concatenate(
        [jnp.concatenate([tile, blank], axis=1), jnp.concatenate([blank, tile], axis=1)], axis=0
    )


def matmul_t(left, right):
    return lax.dot_general(
        left, right, (((1,), (1,)), ((), ())), preferred_element_type=jnp.float32
    )


def planes(nat, flip, rows, cols):
    lanes = nat.shape[2]
    channels = lanes // 2
    identity = (
        lax.broadcasted_iota(jnp.int32, (lanes, lanes), 0)
        == lax.broadcasted_iota(jnp.int32, (lanes, lanes), 1)
    ).astype(jnp.bfloat16)
    moved = [matmul_t(identity, nat[d].astype(jnp.bfloat16)) for d in range(2)]
    for d in range(2):
        for pair in range(rows // 2):
            for low in range(2):
                flip[d, pl.ds(2 * pair + low, channels, stride=rows), :] = moved[d][
                    low * channels:(low + 1) * channels, pair * cols:(pair + 1) * cols
                ]
    return [flip[d].reshape(channels, rows, cols).astype(jnp.bfloat16) for d in range(2)]


def sweep_kernel(
    dims,
    frames_hbm,
    mf_hbm,
    mb_hbm,
    join_hbm,
    conv_ref,
    ahead_ref,
    behind_ref,
    nat,
    frames_ref,
    mf_ref,
    mb_ref,
    join_ref,
    conv_v,
    x_ref,
    flip,
    wj_ref,
    wc_ref,
    mine,
    theirs,
    table_v,
    table_s,
    cand,
    packed,
    landed,
    h_ref,
    z_ref,
    edge_out,
    edge_in,
    m_send,
    f_send,
    f_recv,
    e_send,
    e_recv,
    x_sem,
):
    frame_count, rows, cols, channels, layers, devices = dims
    outs = (ahead_ref, behind_ref)
    lanes = 2 * channels
    half = cols // 2
    bc = cols // BS
    quad = BS // 2
    own_pairs = rows // 2
    margin = layers // 2
    all_pairs = own_pairs + 2 * margin
    cap = bc // (2 * REACH)
    sides = len(OFFSETS)
    lead = BS
    me = lax.axis_index("tiles")

    def present(offset):
        return (me + offset >= 0) & (me + offset < devices)

    def remote(source, target, send, receive, offset):
        return pltpu.make_async_remote_copy(
            src_ref=source,
            dst_ref=target,
            send_sem=send,
            recv_sem=receive,
            device_id={"tiles": me + offset},
            device_id_type=pl.DeviceIdType.MESH,
        )

    def motion_copy(oi, slot):
        return remote(mine, theirs.at[slot], m_send.at[oi], f_recv.at[1, 1, slot], OFFSETS[oi])

    def feature_copy(d, step, oi, slot, offset):
        return remote(
            packed.at[d, step, oi], landed.at[d, step, slot],
            f_send.at[d, oi], f_recv.at[d, step % 2, slot], offset,
        )

    def edge_copy(d, step, side, slot):
        return remote(
            edge_out.at[d, step, side], edge_in.at[d, step, slot],
            e_send.at[d, side], e_recv.at[d, slot], 1 if side else -1,
        )

    first_frames = sorted({0, frame_count - 1})

    def frame_load(f):
        return pltpu.make_async_copy(frames_hbm.at[f], frames_ref.at[f], x_sem.at[f])

    small_loads = [
        pltpu.make_async_copy(source, target, f_send.at[1, k])
        for k, (source, target) in enumerate(
            [(join_hbm, join_ref), (mf_hbm, mf_ref), (mb_hbm, mb_ref)]
        )
    ]
    weight_load = pltpu.make_async_copy(conv_ref, conv_v, f_send.at[0, 0])
    for f in first_frames:
        frame_load(f).start()
    for load in small_loads:
        load.start()
    weight_load.start()
    for f in range(1, frame_count - 1):
        frame_load(f).start()
    barrier = pltpu.get_barrier_semaphore()
    for offset in OFFSETS:
        @pl.when(present(offset))
        def _():
            pl.semaphore_signal(
                barrier, inc=1, device_id={"tiles": me + offset},
                device_id_type=pl.DeviceIdType.MESH,
            )

    for oi, offset in enumerate(OFFSETS):
        @pl.when(jnp.logical_not(present(offset)))
        def _():
            theirs[oi] = jnp.full(mine.shape, -1, jnp.int32)

    for load in small_loads:
        load.wait()
    mine[...] = jnp.zeros(mine.shape, jnp.int32)
    for step in range(frame_count - 1):
        mine[step:step + 1, 0:bc] = mf_ref[step:step + 1, :]
        back = frame_count - 2 - step
        mine[frame_count - 1 + step:frame_count + step, 0:bc] = mb_ref[back:back + 1, :]

    for d in range(2):
        joined = join_ref[d]
        wj_ref[d, :, :lanes] = blockdiag(joined[:, :channels])
        wj_ref[d, :, lanes:] = blockdiag(joined[:, channels:])

    def load_frame(f):
        frame_load(f).wait()
        flip[0] = frames_ref[f].astype(jnp.float32).reshape(channels * rows, cols)
        parts = jnp.concatenate(
            [flip[0, pl.ds(r, channels, stride=rows), :] for r in range(rows)], axis=0
        ).astype(jnp.bfloat16)
        place = lax.broadcasted_iota(jnp.int32, (cols, cols), 0)
        column = lax.broadcasted_iota(jnp.int32, (cols, cols), 1)
        wanted = jnp.where(place < half, 2 * place, 2 * (place - half) + 1)
        moved = matmul_t((column == wanted).astype(jnp.bfloat16), parts).astype(jnp.bfloat16)
        for parity in range(2):
            for pair in range(own_pairs):
                x_ref[f, parity, pair * half:(pair + 1) * half, :] = moved[
                    parity * half:(parity + 1) * half, pair * lanes:(pair + 1) * lanes
                ]

    def build_weights():
        identity = (
            lax.broadcasted_iota(jnp.int32, (channels, channels), 0)
            == lax.broadcasted_iota(jnp.int32, (channels, channels), 1)
        ).astype(jnp.bfloat16)
        low = lax.broadcasted_iota(jnp.int32, (channels, lanes), 1) < channels

        def build_layer(layer, carry):
            for d in range(2):
                wide = jnp.concatenate(
                    [
                        conv_v[d, layer, 3 * down + across]
                        for across in range(3)
                        for down in (1, 0, 2, 1)
                    ],
                    axis=0,
                )
                turned = matmul_t(identity, wide)
                for across in range(3):
                    at = 2 * across * lanes
                    upper_pair = turned[:, at:at + lanes]
                    lower_pair = turned[:, at + lanes:at + 2 * lanes]
                    blocks = [
                        jnp.where(low, pltpu.roll(upper_pair, channels, axis=1), 0.0),
                        upper_pair,
                        lower_pair,
                        jnp.where(low, 0.0, pltpu.roll(lower_pair, channels, axis=1)),
                    ]
                    for k, block in enumerate(blocks):
                        wc_ref[d, layer, across, k * channels:(k + 1) * channels, :] = block.astype(
                            jnp.bfloat16
                        )
            return carry

        lax.fori_loop(0, layers, build_layer, 0)

    def emit(t):
        for d in range(2):
            for pair in range(own_pairs):
                for parity in range(2):
                    nat[d, pl.ds(pair * cols + parity, half, stride=2), :] = cand[
                        d, 2 * pair + parity, lead:lead + half, :
                    ]

        @pl.when(t < frame_count - 1)
        def _():
            for d, plane in enumerate(planes(nat, flip, rows, cols)):
                now = t if d == 0 else frame_count - 1 - t
                outs[d][now] = plane

    table_load = pltpu.make_async_copy(table_v, table_s, m_send.at[0])

    def build_tables():
        for oi, offset in enumerate(OFFSETS):
            @pl.when(present(offset))
            def _():
                motion_copy(oi, oi).wait_send()
                motion_copy(oi, oi).wait_recv()

        depth = mine.shape[0]
        motion = mine[...]
        local = jnp.concatenate(
            [motion - (me + offset) * bc for offset in OFFSETS]
            + [theirs[oi] - me * bc for oi in range(sides)],
            axis=0,
        )
        lane = lax.broadcasted_iota(jnp.int32, local.shape, 1)
        match = (local >= 0) & (local < bc) & (lane < bc)
        flags = match.astype(jnp.int32)
        total = flags
        shift = 1
        while shift < bc:
            total = total + jnp.where(lane >= shift, pltpu.roll(total, shift, axis=1), 0)
            shift *= 2
        rank = total - flags

        mid = sides * depth
        own = motion - me * bc
        picks = jnp.where((own >= 0) & (own < bc), own, 0)
        for oi in range(sides):
            rows_of = slice(oi * depth, (oi + 1) * depth)
            code = bc + oi * cap + jnp.minimum(rank[rows_of], cap - 1)
            picks = picks + jnp.where(match[rows_of], code, 0)
        table_v[sides] = picks * quad

        wanted, order, chosen = local[mid:], rank[mid:], match[mid:]
        values = jnp.concatenate(
            [jnp.where(chosen & (order == slot), wanted, 0) for slot in range(cap)], axis=0
        )
        shift = 1
        while shift < bc + cap:
            values = values + pltpu.roll(values, shift, axis=1)
            shift *= 2
        place = lax.broadcasted_iota(jnp.int32, (mid, mine.shape[1]), 1)
        gathered = jnp.zeros(place.shape, jnp.int32)
        for slot in range(cap):
            gathered = jnp.where(place == bc + slot, values[slot * mid:(slot + 1) * mid], gathered)
        gathered = gathered * quad
        for oi in range(sides):
            table_v[oi] = gathered[oi * depth:(oi + 1) * depth]
        table_load.start()

    upper = lax.broadcasted_iota(jnp.int32, (BS, lanes), 0) < quad

    def two_blocks(d, k, first, second):
        return jnp.where(
            upper,
            cand[d, k, pl.ds(first + lead, BS), :],
            cand[d, k, pl.ds(second + lead - quad, BS), :],
        )

    def activate(d, slot, start, count, even, odd):
        first = start * half
        size = count * half
        z_ref[d, slot, 1, first:first + size, :] = even.astype(jnp.bfloat16)
        z_ref[d, slot, 2, first:first + size, :] = odd.astype(jnp.bfloat16)
        place = lax.broadcasted_iota(jnp.int32, (count, BS, lanes), 1)
        before = pltpu.roll(odd.reshape(count, half, lanes), 1, axis=1)
        before = jnp.concatenate(
            [jnp.where(place == 0, 0.0, before[:, :BS]), before[:, BS:]], axis=1
        )
        z_ref[d, slot, 0, first:first + size, :] = before.reshape(size, lanes).astype(jnp.bfloat16)
        after = pltpu.roll(even.reshape(count, half, lanes), half - 1, axis=1)
        after = jnp.concatenate(
            [after[:, :half - BS], jnp.where(place == BS - 1, 0.0, after[:, half - BS:])], axis=1
        )
        z_ref[d, slot, 3, first:first + size, :] = after.reshape(size, lanes).astype(jnp.bfloat16)

    def send_edges(d, t, first):
        size = own_pairs * half
        edge = margin * half
        for parity in range(2):
            base = parity * size
            edge_out[d, t, 0, parity] = first[base:base + edge]
            edge_out[d, t, 1, parity] = first[base + size - edge:base + size]
        for side in range(2):
            @pl.when(present(1 if side else -1))
            def _():
                edge_copy(d, t, side, 1 - side).start()
        wide = first.astype(jnp.float32)
        h_ref[d, 0, 0, edge:edge + size, :] = wide[:size]
        h_ref[d, 0, 1, edge:edge + size, :] = wide[size:]
        wide = leaky(wide)
        activate(d, 0, margin, own_pairs, wide[:size], wide[size:])

    def begin_first(d):
        now = 0 if d == 0 else frame_count - 1
        both = jnp.concatenate([x_ref[now, 0], x_ref[now, 1]], axis=0)
        send_edges(d, 0, matmul_t(both, wj_ref[d, :, lanes:]).astype(jnp.bfloat16))

    def begin(d, t):
        step = t - 1
        row = d * (frame_count - 1) + step
        for oi, offset in enumerate(OFFSETS):
            @pl.when(present(offset))
            def _():
                feature_copy(d, step, oi, oi, offset).wait_recv()
                at = lead + (bc + oi * cap) * quad
                for k in range(2 * own_pairs):
                    cand[d, k, at:at + cap * quad, :] = landed[d, step, oi, k].astype(jnp.float32)
        picks = [table_s[sides, row, j] for j in range(bc)]
        now = t if d == 0 else frame_count - 1 - t
        parts = []
        for parity in range(2):
            tiles = [
                two_blocks(d, 2 * pair + parity, picks[2 * j], picks[2 * j + 1])
                for pair in range(own_pairs)
                for j in range(bc // 2)
            ]
            taken = jnp.concatenate(tiles, axis=0).astype(jnp.bfloat16)
            parts.append(jnp.concatenate([taken, x_ref[now, parity]], axis=1))
        both = jnp.concatenate(parts, axis=0)
        send_edges(d, t, matmul_t(both, wj_ref[d]).astype(jnp.bfloat16))
        for oi, offset in enumerate(OFFSETS):
            @pl.when(present(offset))
            def _():
                feature_copy(d, step, oi, oi, offset).wait_send()

    top_inside = (me > 0).astype(jnp.float32)
    bottom_inside = (me < devices - 1).astype(jnp.float32)

    low_lanes = lax.broadcasted_iota(jnp.int32, (1, lanes), 1) < channels
    top_mixed = jnp.where(low_lanes, top_inside, 1.0)
    bottom_mixed = jnp.where(low_lanes, 1.0, bottom_inside)

    def inside(value, layer, begin_pair):
        count = value.shape[0] // half
        pieces = []
        for q in range(count):
            start = 2 * (q + begin_pair) + layer + 1 - layers
            piece = value[q * half:(q + 1) * half]
            if start + 1 < 0:
                piece = piece * top_inside
            elif start < 0:
                piece = piece * top_mixed
            elif start >= rows:
                piece = piece * bottom_inside
            elif start + 1 >= rows:
                piece = piece * bottom_mixed
            pieces.append(piece)
        return jnp.concatenate(pieces, axis=0)

    def multiply(d, layer, spans):
        now = layer
        left = jnp.concatenate(
            [
                jnp.concatenate(
                    [
                        z_ref[d, now, k, (first + low) * half:(last + low) * half, :]
                        for k in range(4)
                        for low in range(2)
                    ],
                    axis=1,
                )
                for first, last in spans
            ],
            axis=0,
        )
        taps = [wc_ref[d, layer, across] for across in range(3)]
        blank = jnp.zeros(taps[0].shape, jnp.bfloat16)
        right = jnp.concatenate(
            [
                jnp.concatenate([taps[0], blank], axis=1),
                jnp.concatenate([taps[1], taps[0]], axis=1),
                jnp.concatenate([taps[2], taps[1]], axis=1),
                jnp.concatenate([blank, taps[2]], axis=1),
            ],
            axis=0,
        )
        summed = jnp.dot(left, right, preferred_element_type=jnp.float32)
        parts, at = [], 0
        for first, last in spans:
            parts.append(summed[at:at + (last - first) * half])
            at += (last - first) * half
        return parts

    def run(d, jobs, ahead):
        pending = [multiply(d, *jobs[0])]
        for k, (layer, spans) in enumerate(jobs):
            if k + 1 < len(jobs) and ahead:
                pending.append(multiply(d, *jobs[k + 1]))
            for span, summed in zip(spans, pending[k]):
                settle(d, layer, *span, summed)
            if k + 1 < len(jobs) and not ahead:
                pending.append(multiply(d, *jobs[k + 1]))

    def inner_end(layer):
        return all_pairs - margin - 1 - layer

    def inner(d):
        jobs = [(layer, [(margin, inner_end(layer))]) for layer in range(layers)]
        run(d, [job for job in jobs if job[1][0][1] > margin], False)

    def settle(d, layer, first, last, summed):
        now, later = layer, layer + 1
        count = last - first
        base = first * half
        size = count * half
        first_half = lax.broadcasted_iota(jnp.int32, (size, lanes), 1) < channels
        fresh = []
        for parity in range(2):
            kept = jnp.where(
                first_half,
                h_ref[d, now, parity, base + half:base + half + size, :],
                h_ref[d, now, parity, base:base + size, :],
            )
            fresh.append(
                pltpu.roll(kept, channels, axis=1) + summed[:, parity * lanes:(parity + 1) * lanes]
            )
        if layer < layers - 1:
            for parity in range(2):
                h_ref[d, later, parity, base:base + size, :] = fresh[parity]
            activate(
                d, later, first, count,
                inside(leaky(fresh[0]), layer, first), inside(leaky(fresh[1]), layer, first),
            )
        else:
            for parity in range(2):
                rounded = fresh[parity].astype(jnp.bfloat16).astype(jnp.float32)
                for pair in range(first, last):
                    at = (pair - first) * half
                    cand[d, 2 * pair + parity, lead:lead + half, :] = rounded[at:at + half]

    def send_last(d, t):
        flag = (me // 2) % 2
        oi = (sides - 1) * (1 - flag)
        offset = oi - REACH + (oi + REACH) // (2 * REACH)

        @pl.when(present(offset) & (t < frame_count - 1))
        def _():
            feature_copy(d, t, oi, sides - 1 - oi, offset).start()

    def finish(d, t):
        edge = margin * half
        for side in range(2):
            pair = side * (margin + own_pairs)
            start = pair * half

            @pl.when(present(1 if side else -1))
            def _():
                edge_copy(d, t, side, side).wait_recv()
                even = edge_in[d, t, side, 0].astype(jnp.float32)
                odd = edge_in[d, t, side, 1].astype(jnp.float32)
                h_ref[d, 0, 0, start:start + edge, :] = even
                h_ref[d, 0, 1, start:start + edge, :] = odd
                activate(d, 0, pair, margin, leaky(even), leaky(odd))

            @pl.when(jnp.logical_not(present(1 if side else -1)))
            def _():
                for parity in range(2):
                    h_ref[d, 0, parity, start:start + edge, :] = jnp.zeros((edge, lanes), jnp.float32)
                for k in range(4):
                    z_ref[d, 0, k, start:start + edge, :] = jnp.zeros((edge, lanes), jnp.bfloat16)

        jobs = []
        for layer in range(layers):
            top = (0, margin)
            bottom = (max(margin, inner_end(layer)), all_pairs - 1 - layer)
            jobs += [(layer, [top]), (layer, [bottom])]
        run(d, jobs, True)

        if d == 0:
            @pl.when(t == 0)
            def _():
                table_load.wait()

        @pl.when(t < frame_count - 1)
        def _():
            row = d * (frame_count - 1) + t
            flag = (me // 2) % 2
            for k in range(sides):
                order = (0, 2, 1, 3)[k]
                oi = order + flag * (sides - 1 - 2 * order)
                offset = oi - REACH + (oi + REACH) // (2 * REACH)
                picks = [table_s[oi, row, bc + slot] for slot in range(cap)]
                for tile in range(2 * own_pairs):
                    packed[d, t, oi, tile] = jnp.concatenate(
                        [
                            two_blocks(d, tile, picks[slot], picks[slot + 1])
                            for slot in range(0, cap, 2)
                        ],
                        axis=0,
                    ).astype(jnp.bfloat16)

                if k < sides - 1:
                    @pl.when(present(offset))
                    def _():
                        feature_copy(d, t, oi, sides - 1 - oi, offset).start()

        for side in range(2):
            @pl.when(present(1 if side else -1))
            def _():
                edge_copy(d, t, side, side).wait_send()

    for f in first_frames:
        load_frame(f)

    peers = jnp.minimum(me, REACH) + jnp.minimum(devices - 1 - me, REACH)
    pl.semaphore_wait(barrier, peers)

    for oi, offset in enumerate(OFFSETS):
        @pl.when(present(offset))
        def _():
            motion_copy(oi, sides - 1 - oi).start()
    for d in range(2):
        begin_first(d)

    def load_rest(f, carry):
        load_frame(f)
        return carry

    weight_load.wait()
    build_weights()
    inner(0)
    build_tables()

    def frame_step(t, carry):
        finish(0, t)
        inner(1)
        send_last(0, t)
        finish(1, t)

        @pl.when(t == 0)
        def _():
            lax.fori_loop(1, frame_count - 1, load_rest, 0)

        emit(t)
        send_last(1, t)

        @pl.when(t < frame_count - 1)
        def _():
            begin(0, t + 1)
            inner(0)
            begin(1, t + 1)

        return carry

    lax.fori_loop(0, frame_count, frame_step, 0)


def store_kernel(ahead_ref, behind_ref, nat, ahead_out, behind_out, flip, staged, sems):
    frame_count, channels, rows, cols = ahead_out.shape
    sources, targets = (ahead_ref, behind_ref), (ahead_out, behind_out)
    last = (frame_count - 1, 0)
    copies = [
        pltpu.make_async_copy(sources[d].at[f], targets[d].at[f], sems.at[d, f])
        for d in range(2)
        for f in range(frame_count)
        if f != last[d]
    ]
    for copy in copies:
        copy.start()
    for d, plane in enumerate(planes(nat, flip, rows, cols)):
        staged[d] = plane
    for d in range(2):
        copy = pltpu.make_async_copy(staged.at[d], targets[d].at[last[d]], sems.at[d, last[d]])
        copy.start()
        copies.append(copy)
    for copy in copies:
        copy.wait()


def on_device(frames, motion_forward, motion_backward, join_weight, conv_weight):
    frame_count, channels, rows, cols = frames.shape
    layers = conv_weight.shape[1]
    devices = lax.axis_size("tiles")
    lanes = 2 * channels
    half = cols // 2
    bc = rows // BS * (cols // BS)
    cap = bc // (2 * REACH)
    sides = len(OFFSETS)
    steps = frame_count - 1
    own_pairs = rows // 2
    margin = layers // 2
    all_pairs = own_pairs + 2 * margin
    quad = BS // 2
    reach = 2 * BS + (bc + sides * cap) * quad

    dims = (frame_count, rows, cols, channels, layers, devices)
    vmem = pl.BlockSpec(memory_space=pltpu.VMEM)
    result = pltpu.VMEM(frames.shape, jnp.bfloat16)
    block = (2 * own_pairs, cap * quad, lanes)
    edge = (2, margin * half, lanes)
    swept = pl.pallas_call(
        functools.partial(sweep_kernel, dims),
        out_shape=(result, result, pltpu.VMEM((2, own_pairs * cols, lanes), jnp.float32)),
        in_specs=[pl.BlockSpec(memory_space=pltpu.HBM)] * 5,
        out_specs=(vmem, vmem, vmem),
        scratch_shapes=[
            pltpu.VMEM(frames.shape, jnp.bfloat16),
            pltpu.VMEM(motion_forward.shape, jnp.int32),
            pltpu.VMEM(motion_backward.shape, jnp.int32),
            pltpu.VMEM(join_weight.shape, jnp.bfloat16),
            pltpu.VMEM(conv_weight.shape, jnp.bfloat16),
            pltpu.VMEM((frame_count, 2, own_pairs * half, lanes), jnp.bfloat16),
            pltpu.VMEM((2, channels * rows, cols), jnp.float32),
            pltpu.VMEM((2, lanes, 2 * lanes), jnp.bfloat16),
            pltpu.VMEM((2, layers, 3, 2 * lanes, lanes), jnp.bfloat16),
            pltpu.VMEM((8, 128), jnp.int32),
            pltpu.VMEM((sides, 8, 128), jnp.int32),
            pltpu.VMEM((sides + 1, 8, 128), jnp.int32),
            pltpu.SMEM((sides + 1, 8, 128), jnp.int32),
            pltpu.VMEM((2, 2 * own_pairs, reach, lanes), jnp.float32),
            pltpu.VMEM((2, steps, sides, *block), jnp.bfloat16),
            pltpu.VMEM((2, steps, sides, *block), jnp.bfloat16),
            pltpu.VMEM((2, layers, 2, all_pairs * half, lanes), jnp.float32),
            pltpu.VMEM((2, layers, 4, all_pairs * half, lanes), jnp.bfloat16),
            pltpu.VMEM((2, frame_count, 2, *edge), jnp.bfloat16),
            pltpu.VMEM((2, frame_count, 2, *edge), jnp.bfloat16),
            pltpu.SemaphoreType.DMA((sides,)),
            pltpu.SemaphoreType.DMA((2, sides)),
            pltpu.SemaphoreType.DMA((2, 2, sides)),
            pltpu.SemaphoreType.DMA((2, 2)),
            pltpu.SemaphoreType.DMA((2, 2)),
            pltpu.SemaphoreType.DMA((frame_count,)),
        ],
        compiler_params=pltpu.CompilerParams(
            collective_id=0, has_side_effects=True, vmem_limit_bytes=60 * 1024 * 1024
        ),
    )(frames, motion_forward, motion_backward, join_weight, conv_weight)
    outside = pl.BlockSpec(memory_space=pltpu.HBM)
    plain = jax.ShapeDtypeStruct(frames.shape, jnp.bfloat16)
    return pl.pallas_call(
        store_kernel,
        out_shape=(plain, plain),
        in_specs=[pl.BlockSpec(memory_space=pl.ANY)] * 2 + [vmem],
        out_specs=(outside, outside),
        scratch_shapes=[
            pltpu.VMEM((2, channels * rows, cols), jnp.float32),
            pltpu.VMEM((2, channels, rows, cols), jnp.bfloat16),
            pltpu.SemaphoreType.DMA((2, frame_count)),
        ],
        compiler_params=pltpu.CompilerParams(vmem_limit_bytes=4 * 1024 * 1024),
    )(*swept)


def solution(mesh):
    return jax.shard_map(
        on_device,
        mesh=mesh,
        in_specs=(
            P(None, None, ("clips", "tiles"), None),
            P(None, ("clips", "tiles")),
            P(None, ("clips", "tiles")),
            P(),
            P(),
        ),
        out_specs=(
            P(None, None, ("clips", "tiles"), None),
            P(None, None, ("clips", "tiles"), None),
        ),
        check_vma=False,
    )
```
